128 devices in a mesh: row: 16 (over z_lo, y, core), feat: 8 (over z_hi, x).
Axes of the slice: x: 4, y: 4, z: 4 (z_hi: 2, z_lo: 2; z = z_hi * 2 + z_lo), core: 2. Of those that a mesh axis runs over, the one named last changes fastest.
Arguments:
- features: bfloat16 [16384, 2048], P('row', 'feat'), may hold values from -6 to 6
- cut_points: float32 [2048, 256], P('feat'), as said below
- grad: float32 [16384], P('row'), may hold values from -1 to 1
- hess: float32 [16384], P('row'), may hold values from 0.05 to 0.25
- node_ids: int32 [16384], P('row'), may hold values from 0 to 31
Outputs:
- feature_gain: float32 [2048, 32], P(('feat', 'row'))
- node_best: float32 [32], replicated
The draws below stay inside these ranges and needn't reach their ends.
Inputs may be any that keep to these rules, and one draw needn't show every extreme that they name: Each row of cut_points rises strictly.
All inputs are finite; a program needn't handle non-finite values.
Results may differ from the reference program's by a relative error of at most 0.0065.
Values may be sent and summed in bfloat16 or wider, within the bound.
No kernel may reach another device: no remote copies, remote signals or barrier semaphores. Data moves between devices by JAX's collectives and lax.ppermute only.
A program may use at most 128 MiB of HBM per device.

```python
import math
import jax
import jax.numpy as jnp
from jax import lax

FEATS = 2048
BINS = 256
NODES = 32
ROWS = 16384


def draw_cut_points(key, part):
    first_key, second_key = jax.random.split(jax.random.fold_in(key, 11))
    centre = jax.random.uniform(first_key, (FEATS, 1), jnp.float32, -0.3, 0.3)
    spread = jnp.exp(jax.random.uniform(second_key, (FEATS, 1), jnp.float32, math.log(0.7), math.log(1.4)))
    level = 0.08 + 0.9 * (jnp.arange(BINS, dtype=jnp.float32) + 0.5) / BINS
    quantile = 0.6 * jnp.log(level / (1.0 - level))
    return (centre + spread * quantile[None, :]).astype(jnp.float32)


def set_ends(entries, stream_key, low, high):
    dims = entries.shape
    spot = [jax.random.randint(jax.random.fold_in(stream_key, axis), (), 0, dims[axis]) for axis in range(len(dims))]
    entries = entries.at[tuple(spot)].set(low)
    longest = dims.index(max(dims))
    spot[longest] = (spot[longest] + 1) % dims[longest]
    return entries.at[tuple(spot)].set(high)


def block_levels(key, shape, pieces, smallest, high):
    level, own = 1.0, jax.random.fold_in(key, 6)
    for position, parts in pieces:
        draws = jnp.exp(jax.random.uniform(jax.random.fold_in(own, position), (parts,), jnp.float32, smallest / len(pieces), high / len(pieces)))
        level = level * jnp.repeat(draws, shape[position] // parts).reshape([-1 if axis == position else 1 for axis in range(len(shape))])
    return level


def scatter_about(key, extent, deviation, most, pieces=(), kind=jnp.bfloat16):
    result = jax.random.normal(key, extent, jnp.float32) * deviation
    if len(pieces) > 0:
        result = block_levels(key, extent, pieces, -0.22, 0.18) * result
    return jnp.clip(result, min=-most, max=most).astype(kind)


def setup_inputs(seed: int = 0) -> dict:
    streams_of = jax.random.split(jax.random.key(seed), 6)
    return {
        "features": scatter_about(streams_of[0], (ROWS, FEATS), 1.0, 6.0, ((0, 16), (1, 8))),
        "cut_points": draw_cut_points(jax.random.fold_in(streams_of[5], 71), 0),
        "grad": jnp.clip(jax.random.uniform(streams_of[2], (ROWS,), jnp.float32, -1.0, 1.0) * block_levels(streams_of[2], (ROWS,), ((0, 16),), -0.4, 0.0), -1.0, 1.0),
        "hess": jnp.clip(jnp.exp(math.log(0.25) - 1.609438 * jax.random.uniform(streams_of[3], (ROWS,), jnp.float32) ** block_levels(streams_of[3], (ROWS,), ((0, 16),), -0.2, 0.2)), 0.05, 0.25),
        "node_ids": set_ends(jax.random.randint(streams_of[4], (ROWS,), 0, NODES), jax.random.fold_in(streams_of[4], 1), 0, NODES - 1).astype(jnp.int32),
    }


PENALTY = 1.0


def row_weights(grad, hess, node_ids):
    member = (node_ids[:, None] == jnp.arange(NODES, dtype=jnp.int32)[None, :]).astype(jnp.float32)
    return jnp.concatenate([grad[:, None] * member, hess[:, None] * member], axis=1).astype(jnp.bfloat16)


def split_gains(histogram, totals):
    half = totals.shape[0] // 2
    grad_left = jnp.cumsum(histogram[:, :, :half], axis=1)
    hess_left = jnp.cumsum(histogram[:, :, half:], axis=1)
    grad_total = totals[:half]
    hess_total = totals[half:]
    split_gain = jnp.square(grad_left) / (hess_left + PENALTY)
    split_gain = split_gain + jnp.square(grad_total - grad_left) / (hess_total - hess_left + PENALTY)
    split_gain = split_gain - jnp.square(grad_total) / (hess_total + PENALTY)
    return jnp.max(split_gain, axis=1)


def reference(features, cut_points, grad, hess, node_ids):
    weights = row_weights(grad, hess, node_ids)
    weights_wide = lax.optimization_barrier(weights).astype(jnp.float32)
    totals = jnp.sum(weights_wide, axis=0)

    def per_feature(pair):
        column, edges = pair
        bin_slot = jnp.searchsorted(edges, column.astype(jnp.float32), side="right").astype(jnp.int32)
        return jax.ops.segment_sum(weights_wide, bin_slot, num_segments=BINS + 1)[1:]

    histogram = lax.map(per_feature, (features.T, cut_points))
    feature_gain = split_gains(histogram, totals)
    return feature_gain, jnp.max(feature_gain, axis=0)
```

```python
import functools

import jax
import jax.numpy as jnp
from jax import lax
from jax.experimental import pallas as pl
from jax.experimental.pallas import tpu as pltpu
from jax.sharding import PartitionSpec as P

NODES = 32
PENALTY = 1.0
SWAP = False


def round_up_bf16(edge):
    near = edge.astype(jnp.bfloat16).astype(jnp.float32)
    above = (near + jnp.abs(near) * (0.6 / 128)).astype(jnp.bfloat16).astype(jnp.float32)
    return jnp.where(near < edge, above, near)


def gain_kernel(rows_ref, edge_ref, gain_ref, weight_ref, edge_wide_ref, left_ref):
    groups, _, group_rows = rows_ref.shape
    feats, bins, _ = edge_wide_ref.shape

    for f in range(feats):
        edge_wide_ref[f] = jnp.broadcast_to(
            round_up_bf16(edge_ref[:, f : f + 1]), (bins, 128)
        ).astype(jnp.bfloat16)

    node_column = lax.broadcasted_iota(jnp.int32, (NODES, group_rows), 0).astype(jnp.float32)
    totals = jnp.zeros((2 * NODES, 128), jnp.float32)
    for s in range(groups):
        side = rows_ref[s, feats : feats + 3].astype(jnp.float32)
        member = node_column == side[2:3]
        weights = jnp.concatenate(
            [jnp.where(member, side[0:1], 0.0), jnp.where(member, side[1:2], 0.0)], axis=0
        )
        weight_ref[s] = weights.astype(jnp.bfloat16)

    def one_feature(f):
        edges = jnp.concatenate([edge_wide_ref[f]] * (group_rows // 128), axis=1)
        left_ref[...] = jnp.zeros_like(left_ref)

        @pl.loop(0, groups)
        def _(s):
            value = rows_ref[s, pl.ds(f, 1)]
            below = jnp.where(
                jnp.broadcast_to(value, edges.shape) < edges,
                jnp.bfloat16(1), jnp.bfloat16(0),
            )
            if SWAP:
                left_ref[...] += lax.dot_general(
                    weight_ref[s], below, (((1,), (1,)), ((), ())),
                    preferred_element_type=jnp.float32,
                )
            else:
                left_ref[...] += lax.dot_general(
                    below, weight_ref[s], (((1,), (1,)), ((), ())),
                    preferred_element_type=jnp.float32,
                )
        return left_ref[...]

    ones = jnp.ones((8, group_rows), jnp.bfloat16)
    total = jnp.zeros((8, 2 * NODES), jnp.float32)
    for s in range(groups):
        total = total + lax.dot_general(
            ones, weight_ref[s], (((1,), (1,)), ((), ())), preferred_element_type=jnp.float32
        )
    total = total[0:1]
    grad_total = total[:, :NODES]
    hess_total = total[:, NODES:]
    for f in range(feats):
        below = one_feature(f)
        if SWAP:
            below = below.T
        first = lax.broadcasted_iota(jnp.int32, below.shape, 0) == 0
        left = jnp.where(first, jnp.broadcast_to(total, below.shape), below) - below[0:1]
        grad_left = left[:, :NODES]
        hess_left = left[:, NODES:]
        split = jnp.square(grad_left) / (hess_left + PENALTY)
        split = split + jnp.square(grad_total - grad_left) / (hess_total - hess_left + PENALTY)
        split = split - jnp.square(grad_total) / (hess_total + PENALTY)
        gain_ref[f : f + 1] = jnp.max(split, axis=0, keepdims=True)


def on_device(features, cut_points, grad, hess, node_ids):
    parts = lax.axis_size("row")
    rows, feats = features.shape
    own = feats // parts
    bins = cut_points.shape[1]
    side = jnp.stack(
        [grad.astype(jnp.bfloat16), hess.astype(jnp.bfloat16), node_ids.astype(jnp.bfloat16)]
    )
    sent = jnp.concatenate(
        [features.T.reshape(parts, own, rows), jnp.broadcast_to(side[None], (parts, 3, rows))],
        axis=1,
    )
    gathered = lax.all_to_all(sent, "row", 0, 0)
    edges = lax.dynamic_slice_in_dim(cut_points, lax.axis_index("row") * own, own, 0).T
    feature_gain = pl.pallas_call(
        gain_kernel,
        out_shape=jax.ShapeDtypeStruct((own, NODES), jnp.float32),
        in_specs=[pl.BlockSpec(memory_space=pltpu.VMEM)] * 2,
        out_specs=pl.BlockSpec(memory_space=pltpu.VMEM),
        scratch_shapes=[
            pltpu.VMEM((parts, 2 * NODES, rows), jnp.bfloat16),
            pltpu.VMEM((own, bins, 128), jnp.bfloat16),
            pltpu.VMEM((2 * NODES, bins) if SWAP else (bins, 2 * NODES), jnp.float32),
        ],
        compiler_params=pltpu.CompilerParams(vmem_limit_bytes=40 << 20),
    )(gathered, edges)
    node_best = lax.pmax(jnp.max(feature_gain, axis=0), ("row", "feat"))
    return (feature_gain, node_best)


def solution(mesh):
    placed = (P("row", "feat"), P("feat", None), P("row"), P("row"), P("row"))
    return jax.shard_map(
        on_device,
        mesh=mesh,
        in_specs=placed,
        out_specs=(P(("feat", "row"), None), P()),
        check_vma=False,
    )
```

```python
import jax
import jax.numpy as jnp
from jax import lax
from jax.experimental import pallas as pl
from jax.experimental.pallas import tpu as pltpu
from jax.sharding import PartitionSpec as P

NODES = 32
PENALTY = 1.0
LANES = 128
COARSE = 8
FINE = 32
PIECE = 32


def dot_nt(left, right):
    return lax.dot_general(
        left, right, (((1,), (1,)), ((), ())), preferred_element_type=jnp.float32
    )


def iota(shape, axis):
    return lax.broadcasted_iota(jnp.int32, shape, axis)


def sort_kernel(value_ref, grad_ref, hess_ref, node_ref, sent_ref):
    rows, feats = value_ref.shape
    parts = sent_ref.shape[0]
    own = feats // parts
    chunks = rows // LANES
    node = node_ref[...]
    member = (jnp.broadcast_to(node, (NODES, rows)) == iota((NODES, rows), 0)).astype(jnp.float32)
    earlier = (jnp.broadcast_to(node, (NODES, rows)) < iota((NODES, rows), 0)).astype(jnp.float32)
    upper = (iota((LANES, LANES), 0) <= iota((LANES, LANES), 1)).astype(jnp.bfloat16)
    offset = jnp.sum(earlier, axis=1, keepdims=True)
    ranks = []
    for c in range(chunks):
        piece = member[:, c * LANES : (c + 1) * LANES]
        running = jnp.dot(piece.astype(jnp.bfloat16), upper, preferred_element_type=jnp.float32)
        ranks.append(jnp.sum(piece * (running + (offset - 1.0)), axis=0, keepdims=True))
        offset = offset + jnp.sum(piece, axis=1, keepdims=True)
    rank = jnp.concatenate(ranks, axis=1).astype(jnp.int32)

    side = jnp.concatenate(
        [grad_ref[...], hess_ref[...], node.astype(jnp.float32), jnp.zeros((13, rows), jnp.float32)],
        axis=0,
    ).astype(jnp.bfloat16)
    operand = jnp.concatenate([value_ref[...].T, side], axis=0)
    block = 2 * LANES
    sides = []
    for b in range(rows // block):
        chosen = jnp.where(
            jnp.broadcast_to(rank, (block, rows)) == iota((block, rows), 0) + b * block, 1.0, 0.0
        ).astype(jnp.bfloat16)
        moved = dot_nt(operand, chosen)
        for half in range(2):
            c = 2 * b + half
            lanes = slice(half * LANES, (half + 1) * LANES)
            sent_ref[:, c * own : (c + 1) * own, :] = (
                moved[:feats, lanes].astype(jnp.bfloat16).reshape(parts, own, LANES)
            )
            sides.append(moved[feats : feats + 3, lanes])
    packed = jnp.concatenate(
        [sides[c][i : i + 1] for i in range(3) for c in range(chunks)], axis=0
    ).astype(jnp.bfloat16)
    for d in range(parts):
        sent_ref[d, chunks * own :, :] = packed


def gain_kernel(
    sent_ref, edge_ref, gain_ref, best_ref,
    side_ref, fine_ref, coarse_ref, side_tile_ref, stat_ref, wide_ref, hist_ref, total_ref, top_ref,
):
    parts = sent_ref.shape[0]
    feats, bins = edge_ref.shape
    chunks = (sent_ref.shape[1] - 24) // feats
    per_vector = LANES // PIECE
    tiles, _, tile_rows = fine_ref.shape
    groups = stat_ref.shape[0]
    group_feats = feats // groups

    hist_ref[...] = jnp.zeros_like(hist_ref)
    total_ref[...] = jnp.zeros_like(total_ref)
    for s in range(parts):
        side_ref[s] = sent_ref[s, chunks * feats :, :].astype(jnp.float32)

    edges = edge_ref[...]
    low_edges, high_edges = edges[:, :LANES], edges[:, LANES:]
    lane = iota((feats, LANES), 1)
    coarse_edges = [
        jnp.broadcast_to(edges[:, h * FINE : h * FINE + 1], (feats, LANES)) for h in range(COARSE)
    ]

    def search(value):
        coarse = jnp.full((feats, LANES), -1, jnp.int32)
        for h in range(COARSE):
            coarse = coarse + jnp.where(value >= coarse_edges[h], 1, 0)
        base = jnp.maximum(coarse, 0) * FINE
        is_high = base >= LANES
        base = jnp.where(is_high, base - LANES, base)
        place = base
        step = FINE // 2
        while step >= 1:
            probe = place + step
            edge = jnp.where(
                is_high,
                jnp.take_along_axis(high_edges, probe, axis=1),
                jnp.take_along_axis(low_edges, probe, axis=1),
            )
            place = jnp.where(value >= edge, probe, place)
            step //= 2
        return coarse.astype(jnp.float32), (place - base).astype(jnp.float32)

    block_of = lane // PIECE
    block_row = iota((1, LANES), 1) // PIECE

    def shuffle(pieces, blocks):
        outs = []
        for j in range(per_vector):
            out = None
            for s in range(per_vector):
                shift = ((s - j) * PIECE) % LANES
                moved = pieces[s] if shift == 0 else pltpu.roll(pieces[s], shift, 1)
                out = moved if out is None else jnp.where(blocks == s, moved, out)
            outs.append(out)
        return outs

    @pl.loop(0, chunks)
    def _(c):
        for q in range(parts // per_vector):
            fines, coarses, sides = [], [], []
            for s in range(q * per_vector, (q + 1) * per_vector):
                value = sent_ref[s, pl.ds(pl.multiple_of(c * feats, feats), feats), :].astype(
                    jnp.float32
                )
                coarse, fine = search(value)
                coarses.append(coarse)
                fines.append(fine)
                sides.append([side_ref[s, pl.ds(8 * i + c, 1), :] for i in range(3)])
            lanes = slice(q * LANES, (q + 1) * LANES)
            for j, out in enumerate(shuffle(fines, block_of)):
                fine_ref[c * per_vector + j, :, lanes] = out
            for j, out in enumerate(shuffle(coarses, block_of)):
                coarse_ref[c * per_vector + j, :, lanes] = out
            for i in range(3):
                for j, out in enumerate(shuffle([side[i] for side in sides], block_row)):
                    side_tile_ref[c * per_vector + j, i : i + 1, lanes] = out

    fine_index = iota((FINE, tile_rows), 0).astype(jnp.float32).astype(jnp.bfloat16)
    coarse_index = (iota((2 * COARSE, tile_rows), 0) % COARSE).astype(jnp.float32).astype(jnp.bfloat16)
    is_grad = iota((2 * COARSE, tile_rows), 0) < COARSE
    quarter = iota((2 * COARSE, LANES), 1) // FINE
    zero = jnp.bfloat16(0)
    one = jnp.bfloat16(1)

    @pl.loop(0, tiles)
    def _(t):
        for f in range(feats):
            g, i = f // group_feats, f % group_feats
            fine = fine_ref[t, f : f + 1, :]
            fine = jnp.broadcast_to(fine, (FINE, tile_rows)).astype(jnp.bfloat16)
            stat_ref[g, i * FINE : (i + 1) * FINE, :] = jnp.where(fine <= fine_index, one, zero)
            coarse = coarse_ref[t, f : f + 1, :]
            wide_ref[f] = jnp.broadcast_to(coarse, (2 * COARSE, tile_rows)).astype(jnp.bfloat16)
        grad = side_tile_ref[t, 0:1, :]
        hess = side_tile_ref[t, 1:2, :]
        node = side_tile_ref[t, 2:3, :]
        first = jnp.min(node).astype(jnp.int32)
        last = jnp.max(node).astype(jnp.int32)
        both = jnp.where(
            is_grad,
            jnp.broadcast_to(grad, (2 * COARSE, tile_rows)),
            jnp.broadcast_to(hess, (2 * COARSE, tile_rows)),
        )
        node_wide = jnp.broadcast_to(node, (2 * COARSE, tile_rows))

        @pl.loop(first, last + 1)
        def _(n):
            masked = jnp.where(node_wide == n.astype(jnp.float32), both, 0.0)
            partial = masked[:, :LANES]
            for k in range(1, tile_rows // LANES):
                partial = partial + masked[:, k * LANES : (k + 1) * LANES]
            total_ref[n] += partial
            masked = masked.astype(jnp.bfloat16)
            for g in range(groups):
                stream = jnp.concatenate(
                    [
                        jnp.where(wide_ref[g * group_feats + i] == coarse_index, masked, zero)
                        for i in range(group_feats)
                    ],
                    axis=0,
                )
                product = dot_nt(stream, stat_ref[g])
                for half in range(2):
                    picked = product[64 * half : 64 * half + 64, 128 * half : 128 * half + 128]
                    packed = picked[:16]
                    for i in range(1, 4):
                        packed = jnp.where(quarter == i, picked[16 * i : 16 * i + 16], packed)
                    hist_ref[n, 2 * g + half] += packed

    row = iota((COARSE, LANES), 0)
    last_lane = iota((COARSE, LANES), 1) | (FINE - 1)

    def left_sums(part):
        ends = jnp.take_along_axis(part, last_lane, axis=1)
        shift = 1
        while shift < COARSE:
            ends = ends + jnp.where(row >= shift, pltpu.roll(ends, shift, 0), 0.0)
            shift *= 2
        return part + jnp.where(row >= 1, pltpu.roll(ends, 1, 0), 0.0)

    @pl.loop(0, NODES)
    def _(n):
        sums = jnp.sum(total_ref[n], axis=1, keepdims=True)
        grad_total = jnp.broadcast_to(sums[0:1], (COARSE, LANES))
        hess_total = jnp.broadcast_to(sums[COARSE : COARSE + 1], (COARSE, LANES))
        whole = jnp.square(grad_total) / (hess_total + PENALTY)
        for q in range(feats // 4):
            part = hist_ref[n, q]
            grad_left = left_sums(part[:COARSE])
            hess_left = left_sums(part[COARSE:])
            split = jnp.square(grad_left) / (hess_left + PENALTY)
            split = split + jnp.square(grad_total - grad_left) / (hess_total - hess_left + PENALTY)
            split = split - whole
            top_ref[q, pl.ds(n, 1), :] = jnp.max(split, axis=0, keepdims=True)

    best = None
    for q in range(feats // 4):
        top = top_ref[q]
        shift = FINE // 2
        while shift >= 1:
            top = jnp.maximum(top, pltpu.roll(top, LANES - shift, 1))
            shift //= 2
        turned = top.T
        for i in range(4):
            found = turned[FINE * i : FINE * i + 1]
            gain_ref[4 * q + i : 4 * q + i + 1] = found
            best = found if best is None else jnp.maximum(best, found)
    best_ref[...] = jnp.broadcast_to(best, best_ref.shape)


def on_device(features, cut_points, grad, hess, node_ids):
    parts = lax.axis_size("row")
    others = parts * lax.axis_size("feat")
    rows, feats = features.shape
    own = feats // parts
    bins = cut_points.shape[1]
    length = (own + 3) * rows // LANES
    in_vmem = pl.BlockSpec(memory_space=pltpu.VMEM)
    sent = pl.pallas_call(
        sort_kernel,
        out_shape=jax.ShapeDtypeStruct((parts, length, LANES), jnp.bfloat16),
        in_specs=[in_vmem] * 4,
        out_specs=in_vmem,
        name="sort_rows",
        compiler_params=pltpu.CompilerParams(vmem_limit_bytes=30 << 20),
    )(features, grad[None], hess[None], node_ids[None])
    gathered = lax.all_to_all(sent, "row", 0, 0)
    edges = lax.dynamic_slice_in_dim(cut_points, lax.axis_index("row") * own, own, 0)
    tile_rows = PIECE * parts
    tiles = rows // PIECE
    feature_gain, best = pl.pallas_call(
        gain_kernel,
        out_shape=(
            jax.ShapeDtypeStruct((own, NODES), jnp.float32),
            jax.ShapeDtypeStruct((others, NODES), jnp.float32),
        ),
        in_specs=[in_vmem] * 2,
        out_specs=(in_vmem, in_vmem),
        scratch_shapes=[
            pltpu.VMEM((parts, 24, LANES), jnp.float32),
            pltpu.VMEM((tiles, own, tile_rows), jnp.float32),
            pltpu.VMEM((tiles, own, tile_rows), jnp.float32),
            pltpu.VMEM((tiles, 8, tile_rows), jnp.float32),
            pltpu.VMEM((2, 256, tile_rows), jnp.bfloat16),
            pltpu.VMEM((own, 2 * COARSE, tile_rows), jnp.bfloat16),
            pltpu.VMEM((NODES, own // 4, 2 * COARSE, LANES), jnp.float32),
            pltpu.VMEM((NODES, 2 * COARSE, LANES), jnp.float32),
            pltpu.VMEM((own // 4, NODES, LANES), jnp.float32),
        ],
        name="split_gain",
        compiler_params=pltpu.CompilerParams(vmem_limit_bytes=40 << 20),
    )(gathered, edges)
    node_best = jnp.max(lax.all_to_all(best, ("row", "feat"), 0, 0), axis=0)
    return (feature_gain, node_best)


def solution(mesh):
    placed = (P("row", "feat"), P("feat", None), P("row"), P("row"), P("row"))
    return jax.shard_map(
        on_device,
        mesh=mesh,
        in_specs=placed,
        out_specs=(P(("feat", "row"), None), P()),
        check_vma=False,
    )
```

```python
import jax
import jax.numpy as jnp
from jax import lax
from jax.experimental import pallas as pl
from jax.experimental.pallas import tpu as pltpu
from jax.sharding import PartitionSpec as P

NODES = 32
PENALTY = 1.0
LANES = 128
COARSE = 8
FINE = 32
PIECE = 16
QUAD = 4
NODE_BLOCK = 4
UNROLL = 2


def dot_nt(left, right):
    return lax.dot_general(
        left, right, (((1,), (1,)), ((), ())), preferred_element_type=jnp.float32
    )


def iota(shape, axis):
    return lax.broadcasted_iota(jnp.int32, shape, axis)


def sort_kernel(value_ref, grad_ref, hess_ref, node_ref, sent_ref):
    rows, feats = value_ref.shape
    parts = sent_ref.shape[0]
    own = feats // parts
    chunks = rows // LANES
    node = node_ref[...]
    member = (jnp.broadcast_to(node, (NODES, rows)) == iota((NODES, rows), 0)).astype(jnp.float32)
    earlier = (jnp.broadcast_to(node, (NODES, rows)) < iota((NODES, rows), 0)).astype(jnp.float32)
    upper = (iota((LANES, LANES), 0) <= iota((LANES, LANES), 1)).astype(jnp.bfloat16)
    offset = jnp.sum(earlier, axis=1, keepdims=True)
    ranks = []
    for c in range(chunks):
        piece = member[:, c * LANES : (c + 1) * LANES]
        running = jnp.dot(piece.astype(jnp.bfloat16), upper, preferred_element_type=jnp.float32)
        ranks.append(jnp.sum(piece * (running + (offset - 1.0)), axis=0, keepdims=True))
        offset = offset + jnp.sum(piece, axis=1, keepdims=True)
    rank = jnp.concatenate(ranks, axis=1).astype(jnp.int32)

    side = jnp.concatenate(
        [grad_ref[...], hess_ref[...], node.astype(jnp.float32), jnp.zeros((13, rows), jnp.float32)],
        axis=0,
    ).astype(jnp.bfloat16)
    operand = jnp.concatenate([value_ref[...].T, side], axis=0)
    block = 2 * LANES
    sides = []
    for b in range(rows // block):
        chosen = jnp.where(
            jnp.broadcast_to(rank, (block, rows)) == iota((block, rows), 0) + b * block, 1.0, 0.0
        ).astype(jnp.bfloat16)
        moved = dot_nt(operand, chosen)
        for half in range(2):
            c = 2 * b + half
            lanes = slice(half * LANES, (half + 1) * LANES)
            sent_ref[:, c * own : (c + 1) * own, :] = (
                moved[:feats, lanes].astype(jnp.bfloat16).reshape(parts, own, LANES)
            )
            sides.append(moved[feats : feats + 3, lanes])
    packed = jnp.concatenate(
        [sides[c][i : i + 1] for i in range(3) for c in range(chunks)], axis=0
    ).astype(jnp.bfloat16)
    for d in range(parts):
        sent_ref[d, chunks * own :, :] = packed


def search_tables(edges):
    feats = edges.shape[0]
    lane = iota((feats, LANES), 1)
    low, high = edges[:, :LANES], edges[:, LANES:]

    def pick(index):
        place = jnp.where(index >= LANES, index - LANES, index)
        return jnp.where(
            index >= LANES,
            jnp.take_along_axis(high, place, axis=1),
            jnp.take_along_axis(low, place, axis=1),
        )

    inner = jnp.zeros((feats, LANES), jnp.int32)
    for level in range(7):
        start = 1 << level
        inner = jnp.where(lane >= start, (2 * (lane - start) + 1) * (1 << (7 - level)), inner)
    return pick(inner), pick(2 * lane + 1)


def gain_kernel(
    sent_ref, edge_ref, gain_ref, best_ref,
    side_ref, fine_ref, coarse_ref, side_tile_ref, stat_ref, wide_ref, hist_ref, total_ref, top_ref,
):
    parts = sent_ref.shape[0]
    feats, bins = edge_ref.shape
    chunks = (sent_ref.shape[1] - 24) // feats
    per_vector = LANES // PIECE
    tiles, _, tile_rows = fine_ref.shape
    quads = feats // QUAD

    hist_ref[...] = jnp.zeros_like(hist_ref)
    total_ref[...] = jnp.zeros_like(total_ref)
    for s in range(parts):
        side_ref[s] = sent_ref[s, chunks * feats :, :].astype(jnp.float32)

    edges = edge_ref[...]
    inner, leaf = search_tables(edges)

    def edge_at(j):
        return jnp.broadcast_to(edges[:, j : j + 1], (feats, LANES))

    lowest = edge_at(0)
    steps = [edge_at(32 * h) for h in range(8)]

    def search(value):
        b0 = value >= steps[4]
        b1 = value >= jnp.where(b0, steps[6], steps[2])
        e0 = jnp.where(b1, steps[3], steps[1])
        e1 = jnp.where(b1, steps[7], steps[5])
        b2 = value >= jnp.where(b0, e1, e0)
        place = jnp.where(b0, 12, 8) + jnp.where(b1, 2, 0) + jnp.where(b2, 1, 0)
        for level in range(3, 8):
            if level < 7:
                edge = jnp.take_along_axis(inner, place, axis=1)
            else:
                edge = jnp.take_along_axis(leaf, place - LANES, axis=1)
            place = 2 * place + jnp.where(value >= edge, 1, 0)
        return jnp.where(value >= lowest, place - 256, -1)

    def shuffle(pieces, block):
        pieces = list(pieces)
        step = per_vector // 2
        while step >= 1:
            keep = (block & step) == 0
            for s in range(per_vector):
                if s & step == 0:
                    a, b = pieces[s], pieces[s + step]
                    pieces[s] = jnp.where(keep, a, pltpu.roll(b, step * PIECE, 1))
                    pieces[s + step] = jnp.where(keep, pltpu.roll(a, LANES - step * PIECE, 1), b)
            step //= 2
        return pieces

    block = iota((feats, LANES), 1) // PIECE
    block_side = iota((3, LANES), 1) // PIECE

    @pl.loop(0, chunks)
    def _(c):
        for q in range(parts // per_vector):
            slots, sides = [], []
            for s in range(q * per_vector, (q + 1) * per_vector):
                value = sent_ref[s, pl.ds(pl.multiple_of(c * feats, feats), feats), :]
                slots.append(search(value.astype(jnp.float32)))
                sides.append(side_ref[s, pl.ds(c, 3, stride=8), :])
            lanes = slice(q * LANES, (q + 1) * LANES)
            for j, slot in enumerate(shuffle(slots, block)):
                coarse = slot >> 5
                coarse_ref[c * per_vector + j, :, lanes] = coarse.astype(jnp.float32)
                fine_ref[c * per_vector + j, :, lanes] = (slot & 31).astype(jnp.float32)
            for j, side in enumerate(shuffle(sides, block_side)):
                side_tile_ref[c * per_vector + j, 0:3, lanes] = side

    fine_index = iota((FINE, tile_rows), 0).astype(jnp.float32).astype(jnp.bfloat16)
    coarse_index = (iota((2 * COARSE, tile_rows), 0) & (COARSE - 1)).astype(jnp.float32)
    coarse_index = coarse_index.astype(jnp.bfloat16)
    is_grad = iota((2 * COARSE, tile_rows), 0) < COARSE
    quarter = iota((2 * COARSE, LANES), 1) // FINE
    zero = jnp.bfloat16(0)
    one = jnp.bfloat16(1)
    deep = 2 * COARSE

    def node_block(u, q, first, count, node_wide, both, with_total):
        masked = []
        for b in range(count):
            m = jnp.where(node_wide == (first + b).astype(jnp.float32), both, 0.0)
            if with_total:
                partial = m[:, :LANES]
                for k in range(1, tile_rows // LANES):
                    partial = partial + m[:, k * LANES : (k + 1) * LANES]
                total_ref[first + b] += partial
            masked.append(m.astype(jnp.bfloat16))
        return masked

    def add_product(u, q, first, masked):
        here = [wide_ref[u, q * QUAD + i] == coarse_index for i in range(QUAD)]
        stream = jnp.concatenate(
            [jnp.where(here[i], m, zero) for m in masked for i in range(QUAD)], axis=0
        )
        product = dot_nt(stream, stat_ref[u, q])
        for b in range(len(masked)):
            at = b * QUAD * deep
            packed = product[at : at + deep]
            for i in range(1, QUAD):
                packed = jnp.where(
                    quarter == i, product[at + deep * i : at + deep * (i + 1)], packed
                )
            hist_ref[first + b, q] += packed

    @pl.loop(0, tiles // UNROLL)
    def _(p):
        state = []
        for u in range(UNROLL):
            t = p * UNROLL + u
            grad = side_tile_ref[t, 0:1, :]
            hess = side_tile_ref[t, 1:2, :]
            node = side_tile_ref[t, 2:3, :]
            first = jnp.minimum(jnp.min(node).astype(jnp.int32), NODES - NODE_BLOCK)
            last = jnp.max(node).astype(jnp.int32)
            both = jnp.where(
                is_grad,
                jnp.broadcast_to(grad, (deep, tile_rows)),
                jnp.broadcast_to(hess, (deep, tile_rows)),
            )
            node_wide = jnp.broadcast_to(node, (deep, tile_rows))
            state.append((t, first, last, both, node_wide))
        for u in range(UNROLL):
            t, first, last, both, node_wide = state[u]
            masked = node_block(u, 0, first, NODE_BLOCK, node_wide, both, True)
            for q in range(quads):
                for i in range(QUAD):
                    f = q * QUAD + i
                    fine = jnp.broadcast_to(fine_ref[t, f : f + 1, :], (FINE, tile_rows))
                    stat_ref[u, q, i * FINE : (i + 1) * FINE, :] = jnp.where(
                        fine.astype(jnp.bfloat16) <= fine_index, one, zero
                    )
                    coarse = jnp.broadcast_to(coarse_ref[t, f : f + 1, :], (deep, tile_rows))
                    wide_ref[u, f] = coarse.astype(jnp.bfloat16)
                add_product(u, q, first, masked)
        for u in range(UNROLL):
            t, first, last, both, node_wide = state[u]

            @pl.loop(first + NODE_BLOCK, last + 1)
            def _(n):
                masked = node_block(u, 0, n, 1, node_wide, both, True)
                for q in range(quads):
                    add_product(u, q, n, masked)

    row = iota((COARSE, LANES), 0)
    last_lane = iota((COARSE, LANES), 1) | (FINE - 1)

    def left_sums(part):
        ends = jnp.take_along_axis(part, last_lane, axis=1)
        shift = 1
        while shift < COARSE:
            ends = ends + jnp.where(row >= shift, pltpu.roll(ends, shift, 0), 0.0)
            shift *= 2
        return part + jnp.where(row >= 1, pltpu.roll(ends, 1, 0), 0.0)

    @pl.loop(0, NODES // 2)
    def _(pair):
        for k in range(2):
            n = 2 * pair + k
            sums = jnp.sum(total_ref[n], axis=1, keepdims=True)
            grad_total = jnp.broadcast_to(sums[0:1], (COARSE, LANES))
            hess_total = jnp.broadcast_to(sums[COARSE : COARSE + 1], (COARSE, LANES))
            whole = jnp.square(grad_total) / (hess_total + PENALTY)
            for q in range(quads):
                part = hist_ref[n, q]
                grad_left = left_sums(part[:COARSE])
                hess_left = left_sums(part[COARSE:])
                split = jnp.square(grad_left) / (hess_left + PENALTY)
                split = split + jnp.square(grad_total - grad_left) / (
                    hess_total - hess_left + PENALTY
                )
                split = split - whole
                top_ref[q, pl.ds(n, 1), :] = jnp.max(split, axis=0, keepdims=True)

    best = None
    for q in range(quads):
        top = top_ref[q]
        shift = FINE // 2
        while shift >= 1:
            top = jnp.maximum(top, pltpu.roll(top, LANES - shift, 1))
            shift //= 2
        turned = top.T
        for i in range(QUAD):
            found = turned[FINE * i : FINE * i + 1]
            gain_ref[QUAD * q + i : QUAD * q + i + 1] = found
            best = found if best is None else jnp.maximum(best, found)
    best_ref[...] = jnp.broadcast_to(best, best_ref.shape)


def on_device(features, cut_points, grad, hess, node_ids):
    parts = lax.axis_size("row")
    others = parts * lax.axis_size("feat")
    rows, feats = features.shape
    own = feats // parts
    bins = cut_points.shape[1]
    length = (own + 3) * rows // LANES
    in_vmem = pl.BlockSpec(memory_space=pltpu.VMEM)
    sent = pl.pallas_call(
        sort_kernel,
        out_shape=jax.ShapeDtypeStruct((parts, length, LANES), jnp.bfloat16),
        in_specs=[in_vmem] * 4,
        out_specs=in_vmem,
        name="sort_rows",
        compiler_params=pltpu.CompilerParams(vmem_limit_bytes=30 << 20),
    )(features, grad[None], hess[None], node_ids[None])
    gathered = lax.all_to_all(sent, "row", 0, 0)
    edges = lax.dynamic_slice_in_dim(cut_points, lax.axis_index("row") * own, own, 0)
    tile_rows = PIECE * parts
    tiles = rows // PIECE
    feature_gain, best = pl.pallas_call(
        gain_kernel,
        out_shape=(
            jax.ShapeDtypeStruct((own, NODES), jnp.float32),
            jax.ShapeDtypeStruct((others, NODES), jnp.float32),
        ),
        in_specs=[in_vmem] * 2,
        out_specs=(in_vmem, in_vmem),
        scratch_shapes=[
            pltpu.VMEM((parts, 24, LANES), jnp.float32),
            pltpu.VMEM((tiles, own, tile_rows), jnp.float32),
            pltpu.VMEM((tiles, own, tile_rows), jnp.float32),
            pltpu.VMEM((tiles, 8, tile_rows), jnp.float32),
            pltpu.VMEM((UNROLL, own // QUAD, QUAD * FINE, tile_rows), jnp.bfloat16),
            pltpu.VMEM((UNROLL, own, 2 * COARSE, tile_rows), jnp.bfloat16),
            pltpu.VMEM((NODES, own // QUAD, 2 * COARSE, LANES), jnp.float32),
            pltpu.VMEM((NODES, 2 * COARSE, LANES), jnp.float32),
            pltpu.VMEM((own // QUAD, NODES, LANES), jnp.float32),
        ],
        name="split_gain",
        compiler_params=pltpu.CompilerParams(vmem_limit_bytes=40 << 20),
    )(gathered, edges)
    node_best = jnp.max(lax.all_to_all(best, ("row", "feat"), 0, 0), axis=0)
    return (feature_gain, node_best)


def solution(mesh):
    placed = (P("row", "feat"), P("feat", None), P("row"), P("row"), P("row"))
    return jax.shard_map(
        on_device,
        mesh=mesh,
        in_specs=placed,
        out_specs=(P(("feat", "row"), None), P()),
        check_vma=False,
    )
```

```python
import jax
import jax.numpy as jnp
from jax import lax
from jax.experimental import pallas as pl
from jax.experimental.pallas import tpu as pltpu
from jax.sharding import PartitionSpec as P

NODES = 32
PENALTY = 1.0
LANES = 128
COARSE = 8
FINE = 32
PIECE = 32
QUAD = 4
NODE_BLOCK = 4


def dot_nt(left, right):
    return lax.dot_general(
        left, right, (((1,), (1,)), ((), ())), preferred_element_type=jnp.float32
    )


def iota(shape, axis):
    return lax.broadcasted_iota(jnp.int32, shape, axis)


def look_up(table, index):
    return jnp.take_along_axis(table, index, axis=1, mode="promise_in_bounds")


def sort_kernel(value_ref, grad_ref, hess_ref, node_ref, sent_ref):
    rows, feats = value_ref.shape
    parts = sent_ref.shape[0]
    own = feats // parts
    chunks = rows // LANES
    node = node_ref[...]
    member = (jnp.broadcast_to(node, (NODES, rows)) == iota((NODES, rows), 0)).astype(jnp.float32)
    earlier = (jnp.broadcast_to(node, (NODES, rows)) < iota((NODES, rows), 0)).astype(jnp.float32)
    upper = (iota((LANES, LANES), 0) <= iota((LANES, LANES), 1)).astype(jnp.bfloat16)
    offset = jnp.sum(earlier, axis=1, keepdims=True)
    ranks = []
    for c in range(chunks):
        piece = member[:, c * LANES : (c + 1) * LANES]
        running = jnp.dot(piece.astype(jnp.bfloat16), upper, preferred_element_type=jnp.float32)
        ranks.append(jnp.sum(piece * (running + (offset - 1.0)), axis=0, keepdims=True))
        offset = offset + jnp.sum(piece, axis=1, keepdims=True)
    rank = jnp.concatenate(ranks, axis=1).astype(jnp.int32)

    side = jnp.concatenate(
        [grad_ref[...], hess_ref[...], node.astype(jnp.float32), jnp.zeros((13, rows), jnp.float32)],
        axis=0,
    ).astype(jnp.bfloat16)
    operand = jnp.concatenate([value_ref[...].T, side], axis=0)
    block = 2 * LANES
    sides = []
    for b in range(rows // block):
        chosen = jnp.where(
            jnp.broadcast_to(rank, (block, rows)) == iota((block, rows), 0) + b * block, 1.0, 0.0
        ).astype(jnp.bfloat16)
        moved = dot_nt(operand, chosen)
        for half in range(2):
            c = 2 * b + half
            lanes = slice(half * LANES, (half + 1) * LANES)
            sent_ref[:, c * own : (c + 1) * own, :] = (
                moved[:feats, lanes].astype(jnp.bfloat16).reshape(parts, own, LANES)
            )
            sides.append(moved[feats : feats + 3, lanes])
    packed = jnp.concatenate(
        [sides[c][i : i + 1] for i in range(3) for c in range(chunks)], axis=0
    ).astype(jnp.bfloat16)
    for d in range(parts):
        sent_ref[d, chunks * own :, :] = packed


def search_tables(edges):
    feats = edges.shape[0]
    lane = iota((feats, LANES), 1)
    low, high = edges[:, :LANES], edges[:, LANES:]

    def pick(index):
        place = jnp.where(index >= LANES, index - LANES, index)
        return jnp.where(
            index >= LANES,
            look_up(high, place),
            look_up(low, place),
        )

    inner = jnp.zeros((feats, LANES), jnp.int32)
    for level in range(7):
        start = 1 << level
        inner = jnp.where(lane >= start, (2 * (lane - start) + 1) * (1 << (7 - level)), inner)
    return pick(inner), pick(2 * lane + 1)


def gain_kernel(
    sent_ref, edge_ref, gain_ref, best_ref,
    side_ref, wide_edge_ref, even_fine_ref, even_coarse_ref, even_side_ref,
    odd_fine_ref, odd_coarse_ref, odd_side_ref,
    stat_ref, wide_ref, hist_ref, total_ref, top_ref,
):
    parts = sent_ref.shape[0]
    feats, bins = edge_ref.shape
    chunks = (sent_ref.shape[1] - 24) // feats
    per_vector = LANES // PIECE
    tile_rows = even_fine_ref.shape[2]
    quads = feats // QUAD

    hist_ref[...] = jnp.zeros_like(hist_ref)
    total = jnp.zeros((16, NODES), jnp.float32)
    for s in range(parts):
        side = sent_ref[s, chunks * feats :, :].astype(jnp.float32)
        side_ref[s] = side
        for c in range(0, chunks, 2):
            grad, hess, node = [
                jnp.concatenate([side[8 * i + c : 8 * i + c + 1], side[8 * i + c + 1 : 8 * i + c + 2]], axis=1)
                for i in range(3)
            ]
            wide = (NODES, 2 * LANES)
            member = jnp.where(
                jnp.broadcast_to(node, wide) == iota(wide, 0).astype(jnp.float32), 1.0, 0.0
            ).astype(jnp.bfloat16)
            both = jnp.concatenate(
                [jnp.broadcast_to(grad, (8, 2 * LANES)), jnp.broadcast_to(hess, (8, 2 * LANES))], axis=0
            ).astype(jnp.bfloat16)
            total = total + dot_nt(both, member)
    spread = jnp.concatenate([total, jnp.zeros((16, LANES - NODES), jnp.float32)], axis=1)
    for n in range(NODES):
        total_ref[n] = jnp.broadcast_to(spread[:, n : n + 1], (16, LANES))

    edges = edge_ref[...]
    inner, leaf = search_tables(edges)

    for j in range(32):
        wide_edge_ref[j] = jnp.broadcast_to(edges[:, 8 * j : 8 * j + 1], (feats, LANES))

    def search(value):
        bits = []
        for level in range(5):
            choice = [wide_edge_ref[(2 * m + 1) << (4 - level)] for m in range(1 << level)]
            for bit in reversed(bits):
                choice = [
                    jnp.where(bit, choice[2 * m + 1], choice[2 * m])
                    for m in range(len(choice) // 2)
                ]
            bits.append(value >= choice[0])
        place = jnp.where(bits[0], 48, 32)
        for level in range(1, 5):
            place = place + jnp.where(bits[level], 16 >> level, 0)
        for level in range(5, 8):
            if level < 7:
                edge = look_up(inner, place)
            else:
                edge = look_up(leaf, place - LANES)
            place = place + place + jnp.where(value >= edge, 1, 0)
        return jnp.where(value >= wide_edge_ref[0], place - 256, -1)

    def shuffle(pieces, block):
        pieces = list(pieces)
        step = per_vector // 2
        while step >= 1:
            keep = (block & step) == 0
            for s in range(per_vector):
                if s & step == 0:
                    a, b = pieces[s], pieces[s + step]
                    pieces[s] = jnp.where(keep, a, pltpu.roll(b, step * PIECE, 1))
                    pieces[s + step] = jnp.where(keep, pltpu.roll(a, LANES - step * PIECE, 1), b)
            step //= 2
        return pieces

    block = iota((feats, LANES), 1) // PIECE
    block_side = iota((3, LANES), 1) // PIECE

    def prepare(c, fine_ref, coarse_ref, side_tile_ref):
        for q in range(parts // per_vector):
            slots, sides = [], []
            for s in range(q * per_vector, (q + 1) * per_vector):
                value = sent_ref[s, pl.ds(pl.multiple_of(c * feats, feats), feats), :]
                slots.append(search(value.astype(jnp.float32)))
                sides.append(side_ref[s, pl.ds(c, 3, stride=8), :])
            lanes = slice(q * LANES, (q + 1) * LANES)
            for j, slot in enumerate(shuffle(slots, block)):
                coarse_ref[j, :, lanes] = (slot >> 5).astype(jnp.float32)
                fine_ref[j, :, lanes] = (slot & 31).astype(jnp.float32)
            for j, side in enumerate(shuffle(sides, block_side)):
                side_tile_ref[j, 0:3, lanes] = side

    fine_index = iota((FINE, tile_rows), 0).astype(jnp.float32).astype(jnp.bfloat16)
    coarse_index = (iota((2 * COARSE, tile_rows), 0) & (COARSE - 1)).astype(jnp.float32)
    coarse_index = coarse_index.astype(jnp.bfloat16)
    is_grad = iota((2 * COARSE, tile_rows), 0) < COARSE
    quarter = iota((2 * COARSE, LANES), 1) // FINE
    zero = jnp.bfloat16(0)
    one = jnp.bfloat16(1)
    deep = 2 * COARSE

    def mask_nodes(first, count, node_wide, both):
        return [
            jnp.where(node_wide == (first + b).astype(jnp.float32).astype(jnp.bfloat16), both, zero)
            for b in range(count)
        ]

    def add_product(u, q, first, masked):
        here = [wide_ref[u, q * QUAD + i] for i in range(QUAD)]
        stream = jnp.concatenate([here[i] * m for m in masked for i in range(QUAD)], axis=0)
        product = dot_nt(stream, stat_ref[u, q])
        for b in range(len(masked)):
            at = b * QUAD * deep
            packed = product[at : at + deep]
            for i in range(1, QUAD):
                packed = jnp.where(
                    quarter == i, product[at + deep * i : at + deep * (i + 1)], packed
                )
            hist_ref[first + b, q] += packed

    def tile_sides(side_tile_ref, u):
        wide = (deep, tile_rows)
        both = jnp.where(
            is_grad,
            jnp.broadcast_to(side_tile_ref[u, 0:1, :], wide),
            jnp.broadcast_to(side_tile_ref[u, 1:2, :], wide),
        ).astype(jnp.bfloat16)
        node = side_tile_ref[u, 2:3, :]
        return node, jnp.broadcast_to(node, wide).astype(jnp.bfloat16), both

    def accumulate(fine_ref, coarse_ref, side_tile_ref):
        ranges = []
        for u in range(per_vector):
            node = side_tile_ref[u, 2:3, :]
            first = jnp.minimum(jnp.min(node).astype(jnp.int32), NODES - NODE_BLOCK)
            ranges.append((first, jnp.max(node).astype(jnp.int32)))
        for u in range(per_vector):
            node, node_wide, both = tile_sides(side_tile_ref, u)
            masked = mask_nodes(ranges[u][0], NODE_BLOCK, node_wide, both)
            for q in range(quads):
                for i in range(QUAD):
                    f = q * QUAD + i
                    fine = jnp.broadcast_to(fine_ref[u, f : f + 1, :], (FINE, tile_rows))
                    stat_ref[u, q, i * FINE : (i + 1) * FINE, :] = jnp.where(
                        fine.astype(jnp.bfloat16) <= fine_index, one, zero
                    )
                    coarse = jnp.broadcast_to(coarse_ref[u, f : f + 1, :], (deep, tile_rows))
                    wide_ref[u, f] = jnp.where(
                        coarse.astype(jnp.bfloat16) == coarse_index, one, zero
                    )
                add_product(u, q, ranges[u][0], masked)
        return ranges

    def accumulate_rest(ranges, side_tile_ref):
        for u in range(per_vector):
            first, last = ranges[u]

            @pl.loop(first + NODE_BLOCK, last + 1)
            def _(n):
                node, node_wide, both = tile_sides(side_tile_ref, u)
                masked = mask_nodes(n, 1, node_wide, both)
                for q in range(quads):
                    add_product(u, q, n, masked)

    even = (even_fine_ref, even_coarse_ref, even_side_ref)
    odd = (odd_fine_ref, odd_coarse_ref, odd_side_ref)
    prepare(0, *even)

    @pl.loop(0, chunks // 2)
    def _(pair):
        ranges = accumulate(*even)
        prepare(2 * pair + 1, *odd)
        accumulate_rest(ranges, even_side_ref)
        ranges = accumulate(*odd)
        prepare(jnp.minimum(2 * pair + 2, chunks - 1), *even)
        accumulate_rest(ranges, odd_side_ref)

    row = iota((COARSE, LANES), 0)
    last_lane = iota((COARSE, LANES), 1) | (FINE - 1)

    def left_sums(part):
        ends = look_up(part, last_lane)
        shift = 1
        while shift < COARSE:
            ends = ends + jnp.where(row >= shift, pltpu.roll(ends, shift, 0), 0.0)
            shift *= 2
        return part + jnp.where(row >= 1, pltpu.roll(ends, 1, 0), 0.0)

    @pl.loop(0, NODES // 4)
    def _(group):
        for k in range(4):
            n = 4 * group + k
            grad_total = total_ref[n, :COARSE]
            hess_total = total_ref[n, COARSE:]
            whole = jnp.square(grad_total) / (hess_total + PENALTY)
            for q in range(quads):
                part = hist_ref[n, q]
                grad_left = left_sums(part[:COARSE])
                hess_left = left_sums(part[COARSE:])
                split = jnp.square(grad_left) / (hess_left + PENALTY)
                split = split + jnp.square(grad_total - grad_left) / (
                    hess_total - hess_left + PENALTY
                )
                split = split - whole
                top_ref[q, pl.ds(n, 1), :] = jnp.max(split, axis=0, keepdims=True)

    best = None
    for q in range(quads):
        top = top_ref[q]
        shift = FINE // 2
        while shift >= 1:
            top = jnp.maximum(top, pltpu.roll(top, LANES - shift, 1))
            shift //= 2
        turned = top.T
        for i in range(QUAD):
            found = turned[FINE * i : FINE * i + 1]
            gain_ref[QUAD * q + i : QUAD * q + i + 1] = found
            best = found if best is None else jnp.maximum(best, found)
    best_ref[...] = jnp.broadcast_to(best, best_ref.shape)


def on_device(features, cut_points, grad, hess, node_ids):
    parts = lax.axis_size("row")
    others = parts * lax.axis_size("feat")
    rows, feats = features.shape
    own = feats // parts
    bins = cut_points.shape[1]
    length = (own + 3) * rows // LANES
    in_vmem = pl.BlockSpec(memory_space=pltpu.VMEM)
    sent = pl.pallas_call(
        sort_kernel,
        out_shape=jax.ShapeDtypeStruct((parts, length, LANES), jnp.bfloat16),
        in_specs=[in_vmem] * 4,
        out_specs=in_vmem,
        name="sort_rows",
        compiler_params=pltpu.CompilerParams(vmem_limit_bytes=30 << 20),
    )(features, grad[None], hess[None], node_ids[None])
    gathered = lax.all_to_all(sent, "row", 0, 0)
    edges = lax.dynamic_slice_in_dim(cut_points, lax.axis_index("row") * own, own, 0)
    tile_rows = PIECE * parts
    feature_gain, best = pl.pallas_call(
        gain_kernel,
        out_shape=(
            jax.ShapeDtypeStruct((own, NODES), jnp.float32),
            jax.ShapeDtypeStruct((others, NODES), jnp.float32),
        ),
        in_specs=[in_vmem] * 2,
        out_specs=(in_vmem, in_vmem),
        scratch_shapes=[
            pltpu.VMEM((parts, 24, LANES), jnp.float32),
            pltpu.VMEM((32, own, LANES), jnp.float32),
            *[
                pltpu.VMEM((LANES // PIECE, height, tile_rows), jnp.float32)
                for height in (own, own, 8, own, own, 8)
            ],
            pltpu.VMEM((LANES // PIECE, own // QUAD, QUAD * FINE, tile_rows), jnp.bfloat16),
            pltpu.VMEM((LANES // PIECE, own, 2 * COARSE, tile_rows), jnp.bfloat16),
            pltpu.VMEM((NODES, own // QUAD, 2 * COARSE, LANES), jnp.float32),
            pltpu.VMEM((NODES, 2 * COARSE, LANES), jnp.float32),
            pltpu.VMEM((own // QUAD, NODES, LANES), jnp.float32),
        ],
        name="split_gain",
        compiler_params=pltpu.CompilerParams(vmem_limit_bytes=40 << 20),
    )(gathered, edges)
    node_best = jnp.max(lax.all_to_all(best, ("row", "feat"), 0, 0), axis=0)
    return (feature_gain, node_best)


def solution(mesh):
    placed = (P("row", "feat"), P("feat", None), P("row"), P("row"), P("row"))
    return jax.shard_map(
        on_device,
        mesh=mesh,
        in_specs=placed,
        out_specs=(P(("feat", "row"), None), P()),
        check_vma=False,
    )
```

```python
import jax
import jax.numpy as jnp
from jax import lax
from jax.experimental import pallas as pl
from jax.experimental.pallas import tpu as pltpu
from jax.sharding import PartitionSpec as P

NODES = 32
PENALTY = 1.0
LANES = 128
COARSE = 8
FINE = 32
PIECE = 32
QUAD = 4
NODE_BLOCK = 4


def dot_nt(left, right):
    return lax.dot_general(
        left, right, (((1,), (1,)), ((), ())), preferred_element_type=jnp.float32
    )


def iota(shape, axis):
    return lax.broadcasted_iota(jnp.int32, shape, axis)


def look_up(table, index):
    return jnp.take_along_axis(table, index, axis=1, mode="promise_in_bounds")


def sort_kernel(
    value_in, grad_in, hess_in, node_in, sent_ref, value_ref, grad_ref, hess_ref, node_ref, arrived
):
    pairs = ((node_in, node_ref), (grad_in, grad_ref), (hess_in, hess_ref), (value_in, value_ref))
    copies = [
        pltpu.make_async_copy(source, target, arrived.at[k])
        for k, (source, target) in enumerate(pairs)
    ]
    for copy in copies:
        copy.start()
    rows, feats = value_ref.shape
    parts = sent_ref.shape[0]
    own = feats // parts
    chunks = rows // LANES
    copies[0].wait()
    node = node_ref[...]
    member = (jnp.broadcast_to(node, (NODES, rows)) == iota((NODES, rows), 0)).astype(jnp.float32)
    earlier = (jnp.broadcast_to(node, (NODES, rows)) < iota((NODES, rows), 0)).astype(jnp.float32)
    upper = (iota((LANES, LANES), 0) <= iota((LANES, LANES), 1)).astype(jnp.bfloat16)
    offset = jnp.sum(earlier, axis=1, keepdims=True)
    ranks = []
    for c in range(chunks):
        piece = member[:, c * LANES : (c + 1) * LANES]
        running = jnp.dot(piece.astype(jnp.bfloat16), upper, preferred_element_type=jnp.float32)
        ranks.append(jnp.sum(piece * (running + (offset - 1.0)), axis=0, keepdims=True))
        offset = offset + jnp.sum(piece, axis=1, keepdims=True)
    rank = jnp.concatenate(ranks, axis=1).astype(jnp.int32)

    for copy in copies[1:]:
        copy.wait()
    side = jnp.concatenate(
        [grad_ref[...], hess_ref[...], node.astype(jnp.float32), jnp.zeros((13, rows), jnp.float32)],
        axis=0,
    ).astype(jnp.bfloat16)
    operand = jnp.concatenate([value_ref[...].T, side], axis=0)
    block = 2 * LANES
    sides = []
    for b in range(rows // block):
        chosen = jnp.where(
            jnp.broadcast_to(rank, (block, rows)) == iota((block, rows), 0) + b * block, 1.0, 0.0
        ).astype(jnp.bfloat16)
        moved = dot_nt(operand, chosen)
        for half in range(2):
            c = 2 * b + half
            lanes = slice(half * LANES, (half + 1) * LANES)
            sent_ref[:, c * own : (c + 1) * own, :] = (
                moved[:feats, lanes].astype(jnp.bfloat16).reshape(parts, own, LANES)
            )
            sides.append(moved[feats : feats + 3, lanes])
    packed = jnp.concatenate(
        [sides[c][i : i + 1] for i in range(3) for c in range(chunks)], axis=0
    ).astype(jnp.bfloat16)
    for d in range(parts):
        sent_ref[d, chunks * own :, :] = packed


def search_tables(edges):
    feats = edges.shape[0]
    lane = iota((feats, LANES), 1)
    low, high = edges[:, :LANES], edges[:, LANES:]

    def pick(index):
        place = jnp.where(index >= LANES, index - LANES, index)
        return jnp.where(
            index >= LANES,
            look_up(high, place),
            look_up(low, place),
        )

    inner = jnp.zeros((feats, LANES), jnp.int32)
    for level in range(7):
        start = 1 << level
        inner = jnp.where(lane >= start, (2 * (lane - start) + 1) * (1 << (7 - level)), inner)
    return pick(inner), pick(2 * lane + 1)


def gain_kernel(
    sent_ref, edge_ref, gain_ref, best_ref,
    side_ref, wide_edge_ref, even_fine_ref, even_coarse_ref, even_side_ref,
    odd_fine_ref, odd_coarse_ref, odd_side_ref,
    stat_ref, wide_ref, hist_ref, total_ref, top_ref,
):
    parts = sent_ref.shape[0]
    feats, bins = edge_ref.shape
    chunks = (sent_ref.shape[1] - 24) // feats
    per_vector = LANES // PIECE
    tile_rows = even_fine_ref.shape[2]
    quads = feats // QUAD

    hist_ref[...] = jnp.zeros_like(hist_ref)
    total = jnp.zeros((16, NODES), jnp.float32)
    for s in range(parts):
        side = sent_ref[s, chunks * feats :, :].astype(jnp.float32)
        side_ref[s] = side
        for c in range(0, chunks, 2):
            grad, hess, node = [
                jnp.concatenate([side[8 * i + c : 8 * i + c + 1], side[8 * i + c + 1 : 8 * i + c + 2]], axis=1)
                for i in range(3)
            ]
            wide = (NODES, 2 * LANES)
            member = jnp.where(
                jnp.broadcast_to(node, wide).astype(jnp.bfloat16)
                == iota(wide, 0).astype(jnp.float32).astype(jnp.bfloat16),
                jnp.bfloat16(1),
                jnp.bfloat16(0),
            )
            both = jnp.concatenate(
                [jnp.broadcast_to(grad, (8, 2 * LANES)), jnp.broadcast_to(hess, (8, 2 * LANES))], axis=0
            ).astype(jnp.bfloat16)
            total = total + dot_nt(both, member)
    spread = jnp.concatenate([total, jnp.zeros((16, LANES - NODES), jnp.float32)], axis=1)
    for n in range(NODES):
        total_ref[n] = jnp.broadcast_to(spread[:, n : n + 1], (16, LANES))

    edges = edge_ref[...]
    inner, leaf = search_tables(edges)

    for j in range(8):
        wide_edge_ref[j] = jnp.broadcast_to(edges[:, 32 * j : 32 * j + 1], (feats, LANES))

    def search(value):
        bits = []
        for level in range(3):
            choice = [wide_edge_ref[(2 * m + 1) << (2 - level)] for m in range(1 << level)]
            for bit in reversed(bits):
                choice = [
                    jnp.where(bit, choice[2 * m + 1], choice[2 * m])
                    for m in range(len(choice) // 2)
                ]
            bits.append(value >= choice[0])
        place = jnp.where(bits[0], 12, 8)
        for level in range(1, 3):
            place = place + jnp.where(bits[level], 4 >> level, 0)
        for level in range(3, 8):
            if level < 7:
                edge = look_up(inner, place)
            else:
                edge = look_up(leaf, place - LANES)
            place = place + place + jnp.where(value >= edge, 1, 0)
        return jnp.where(value >= wide_edge_ref[0], place - 256, -1)

    def shuffle(pieces, block):
        pieces = list(pieces)
        step = per_vector // 2
        while step >= 1:
            keep = (block & step) == 0
            for s in range(per_vector):
                if s & step == 0:
                    a, b = pieces[s], pieces[s + step]
                    pieces[s] = jnp.where(keep, a, pltpu.roll(b, step * PIECE, 1))
                    pieces[s + step] = jnp.where(keep, pltpu.roll(a, LANES - step * PIECE, 1), b)
            step //= 2
        return pieces

    block = iota((feats, LANES), 1) // PIECE
    block_side = iota((3, LANES), 1) // PIECE

    def prepare(c, fine_ref, coarse_ref, side_tile_ref):
        for q in range(parts // per_vector):
            slots, sides = [], []
            for s in range(q * per_vector, (q + 1) * per_vector):
                value = sent_ref[s, pl.ds(pl.multiple_of(c * feats, feats), feats), :]
                slots.append(search(value.astype(jnp.float32)))
                sides.append(side_ref[s, pl.ds(c, 3, stride=8), :])
            lanes = slice(q * LANES, (q + 1) * LANES)
            for j, slot in enumerate(shuffle(slots, block)):
                coarse_ref[j, :, lanes] = (slot >> 5).astype(jnp.float32)
                fine_ref[j, :, lanes] = (slot & 31).astype(jnp.float32)
            for j, side in enumerate(shuffle(sides, block_side)):
                side_tile_ref[j, 0:3, lanes] = side

    fine_index = iota((FINE, tile_rows), 0).astype(jnp.float32).astype(jnp.bfloat16)
    coarse_index = (iota((2 * COARSE, tile_rows), 0) & (COARSE - 1)).astype(jnp.float32)
    coarse_index = coarse_index.astype(jnp.bfloat16)
    is_grad = iota((2 * COARSE, tile_rows), 0) < COARSE
    quarter = iota((2 * COARSE, LANES), 1) // FINE
    zero = jnp.bfloat16(0)
    one = jnp.bfloat16(1)
    deep = 2 * COARSE

    def mask_nodes(first, count, node_wide, both):
        return [
            jnp.where(node_wide == (first + b).astype(jnp.float32).astype(jnp.bfloat16), both, zero)
            for b in range(count)
        ]

    def add_product(u, q, first, masked):
        here = [wide_ref[u, q * QUAD + i] for i in range(QUAD)]
        stream = jnp.concatenate([here[i] * m for m in masked for i in range(QUAD)], axis=0)
        product = dot_nt(stream, stat_ref[u, q])
        for b in range(len(masked)):
            at = b * QUAD * deep
            packed = product[at : at + deep]
            for i in range(1, QUAD):
                packed = jnp.where(
                    quarter == i, product[at + deep * i : at + deep * (i + 1)], packed
                )
            hist_ref[first + b, q] += packed

    def tile_sides(side_tile_ref, u):
        wide = (deep, tile_rows)
        both = jnp.where(
            is_grad,
            jnp.broadcast_to(side_tile_ref[u, 0:1, :], wide),
            jnp.broadcast_to(side_tile_ref[u, 1:2, :], wide),
        ).astype(jnp.bfloat16)
        node = side_tile_ref[u, 2:3, :]
        return node, jnp.broadcast_to(node, wide).astype(jnp.bfloat16), both

    def accumulate(fine_ref, coarse_ref, side_tile_ref):
        ranges = []
        for u in range(per_vector):
            node = side_tile_ref[u, 2:3, :]
            first = jnp.minimum(jnp.min(node).astype(jnp.int32), NODES - NODE_BLOCK)
            ranges.append((first, jnp.max(node).astype(jnp.int32)))
        for u in range(per_vector):
            node, node_wide, both = tile_sides(side_tile_ref, u)
            masked = mask_nodes(ranges[u][0], NODE_BLOCK, node_wide, both)
            for q in range(quads):
                for i in range(QUAD):
                    f = q * QUAD + i
                    fine = jnp.broadcast_to(fine_ref[u, f : f + 1, :], (FINE, tile_rows))
                    stat_ref[u, q, i * FINE : (i + 1) * FINE, :] = jnp.where(
                        fine.astype(jnp.bfloat16) <= fine_index, one, zero
                    )
                    coarse = jnp.broadcast_to(coarse_ref[u, f : f + 1, :], (deep, tile_rows))
                    wide_ref[u, f] = jnp.where(
                        coarse.astype(jnp.bfloat16) == coarse_index, one, zero
                    )
                add_product(u, q, ranges[u][0], masked)
        return ranges

    def accumulate_rest(ranges, side_tile_ref):
        for u in range(per_vector):
            first, last = ranges[u]

            @pl.loop(first + NODE_BLOCK, last + 1)
            def _(n):
                node, node_wide, both = tile_sides(side_tile_ref, u)
                masked = mask_nodes(n, 1, node_wide, both)
                for q in range(quads):
                    add_product(u, q, n, masked)

    even = (even_fine_ref, even_coarse_ref, even_side_ref)
    odd = (odd_fine_ref, odd_coarse_ref, odd_side_ref)
    prepare(0, *even)

    @pl.loop(0, chunks // 2)
    def _(pair):
        ranges = accumulate(*even)
        prepare(2 * pair + 1, *odd)
        accumulate_rest(ranges, even_side_ref)
        ranges = accumulate(*odd)
        prepare(jnp.minimum(2 * pair + 2, chunks - 1), *even)
        accumulate_rest(ranges, odd_side_ref)

    row = iota((COARSE, LANES), 0)
    last_lane = iota((COARSE, LANES), 1) | (FINE - 1)

    def left_sums(part):
        ends = look_up(part, last_lane)
        shift = 1
        while shift < COARSE:
            ends = ends + jnp.where(row >= shift, pltpu.roll(ends, shift, 0), 0.0)
            shift *= 2
        return part + jnp.where(row >= 1, pltpu.roll(ends, 1, 0), 0.0)

    @pl.loop(0, NODES // 4)
    def _(group):
        for k in range(4):
            n = 4 * group + k
            grad_total = total_ref[n, :COARSE]
            hess_total = total_ref[n, COARSE:]
            whole = jnp.square(grad_total) / (hess_total + PENALTY)
            for q in range(quads):
                part = hist_ref[n, q]
                grad_left = left_sums(part[:COARSE])
                hess_left = left_sums(part[COARSE:])
                split = jnp.square(grad_left) / (hess_left + PENALTY)
                split = split + jnp.square(grad_total - grad_left) / (
                    hess_total - hess_left + PENALTY
                )
                split = split - whole
                top_ref[q, pl.ds(n, 1), :] = jnp.max(split, axis=0, keepdims=True)

    best = None
    for q in range(quads):
        top = top_ref[q]
        shift = FINE // 2
        while shift >= 1:
            top = jnp.maximum(top, pltpu.roll(top, LANES - shift, 1))
            shift //= 2
        turned = top.T
        for i in range(QUAD):
            found = turned[FINE * i : FINE * i + 1]
            gain_ref[QUAD * q + i : QUAD * q + i + 1] = found
            best = found if best is None else jnp.maximum(best, found)
    best_ref[...] = jnp.broadcast_to(best, best_ref.shape)


def on_device(features, cut_points, grad, hess, node_ids):
    parts = lax.axis_size("row")
    others = parts * lax.axis_size("feat")
    rows, feats = features.shape
    own = feats // parts
    bins = cut_points.shape[1]
    length = (own + 3) * rows // LANES
    in_vmem = pl.BlockSpec(memory_space=pltpu.VMEM)
    sent = pl.pallas_call(
        sort_kernel,
        out_shape=jax.ShapeDtypeStruct((parts, length, LANES), jnp.bfloat16),
        in_specs=[pl.BlockSpec(memory_space=pltpu.MemorySpace.HBM)] * 4,
        out_specs=in_vmem,
        scratch_shapes=[
            pltpu.VMEM((rows, feats), jnp.bfloat16),
            pltpu.VMEM((1, rows), jnp.float32),
            pltpu.VMEM((1, rows), jnp.float32),
            pltpu.VMEM((1, rows), jnp.int32),
            pltpu.SemaphoreType.DMA((4,)),
        ],
        name="sort_rows",
        compiler_params=pltpu.CompilerParams(vmem_limit_bytes=30 << 20),
    )(features, grad[None], hess[None], node_ids[None])
    gathered = lax.all_to_all(sent, "row", 0, 0)
    edges = lax.dynamic_slice_in_dim(cut_points, lax.axis_index("row") * own, own, 0)
    tile_rows = PIECE * parts
    feature_gain, best = pl.pallas_call(
        gain_kernel,
        out_shape=(
            jax.ShapeDtypeStruct((own, NODES), jnp.float32),
            jax.ShapeDtypeStruct((others, NODES), jnp.float32),
        ),
        in_specs=[in_vmem] * 2,
        out_specs=(in_vmem, in_vmem),
        scratch_shapes=[
            pltpu.VMEM((parts, 24, LANES), jnp.float32),
            pltpu.VMEM((8, own, LANES), jnp.float32),
            *[
                pltpu.VMEM((LANES // PIECE, height, tile_rows), jnp.float32)
                for height in (own, own, 8, own, own, 8)
            ],
            pltpu.VMEM((LANES // PIECE, own // QUAD, QUAD * FINE, tile_rows), jnp.bfloat16),
            pltpu.VMEM((LANES // PIECE, own, 2 * COARSE, tile_rows), jnp.bfloat16),
            pltpu.VMEM((NODES, own // QUAD, 2 * COARSE, LANES), jnp.float32),
            pltpu.VMEM((NODES, 2 * COARSE, LANES), jnp.float32),
            pltpu.VMEM((own // QUAD, NODES, LANES), jnp.float32),
        ],
        name="split_gain",
        compiler_params=pltpu.CompilerParams(vmem_limit_bytes=40 << 20),
    )(gathered, edges)
    node_best = jnp.max(lax.all_to_all(best, ("row", "feat"), 0, 0), axis=0)
    return (feature_gain, node_best)


def solution(mesh):
    placed = (P("row", "feat"), P("feat", None), P("row"), P("row"), P("row"))
    return jax.shard_map(
        on_device,
        mesh=mesh,
        in_specs=placed,
        out_specs=(P(("feat", "row"), None), P()),
        check_vma=False,
    )
```

```python
import jax
import jax.numpy as jnp
from jax import lax
from jax.experimental import pallas as pl
from jax.experimental.pallas import tpu as pltpu
from jax.sharding import PartitionSpec as P

NODES = 32
PENALTY = 1.0
LANES = 128
COARSE = 8
FINE = 32
PIECE = 32
QUAD = 4
NODE_BLOCK = 4


def dot_nt(left, right):
    return lax.dot_general(
        left, right, (((1,), (1,)), ((), ())), preferred_element_type=jnp.float32
    )


def iota(shape, axis):
    return lax.broadcasted_iota(jnp.int32, shape, axis)


def look_up(table, index):
    return jnp.take_along_axis(table, index, axis=1, mode="promise_in_bounds")


def sort_kernel(
    value_in, grad_in, hess_in, node_in, sent_ref, value_ref, grad_ref, hess_ref, node_ref, arrived
):
    pairs = ((node_in, node_ref), (grad_in, grad_ref), (hess_in, hess_ref), (value_in, value_ref))
    copies = [
        pltpu.make_async_copy(source, target, arrived.at[k])
        for k, (source, target) in enumerate(pairs)
    ]
    for copy in copies:
        copy.start()
    rows, feats = value_ref.shape
    parts = sent_ref.shape[0]
    own = feats // parts
    chunks = rows // LANES
    copies[0].wait()
    node = node_ref[...]
    member = (jnp.broadcast_to(node, (NODES, rows)) == iota((NODES, rows), 0)).astype(jnp.float32)
    earlier = (jnp.broadcast_to(node, (NODES, rows)) < iota((NODES, rows), 0)).astype(jnp.float32)
    upper = (iota((LANES, LANES), 0) <= iota((LANES, LANES), 1)).astype(jnp.bfloat16)
    offset = jnp.sum(earlier, axis=1, keepdims=True)
    ranks = []
    for c in range(chunks):
        piece = member[:, c * LANES : (c + 1) * LANES]
        running = jnp.dot(piece.astype(jnp.bfloat16), upper, preferred_element_type=jnp.float32)
        ranks.append(jnp.sum(piece * (running + (offset - 1.0)), axis=0, keepdims=True))
        offset = offset + jnp.sum(piece, axis=1, keepdims=True)
    rank = jnp.concatenate(ranks, axis=1).astype(jnp.int32)

    for copy in copies[1:]:
        copy.wait()
    side = jnp.concatenate(
        [grad_ref[...], hess_ref[...], node.astype(jnp.float32), jnp.zeros((13, rows), jnp.float32)],
        axis=0,
    ).astype(jnp.bfloat16)
    operand = jnp.concatenate([value_ref[...].T, side], axis=0)
    block = 2 * LANES
    sides = []
    for b in range(rows // block):
        chosen = jnp.where(
            jnp.broadcast_to(rank, (block, rows)) == iota((block, rows), 0) + b * block, 1.0, 0.0
        ).astype(jnp.bfloat16)
        moved = dot_nt(operand, chosen)
        for half in range(2):
            c = 2 * b + half
            lanes = slice(half * LANES, (half + 1) * LANES)
            sent_ref[:, c * own : (c + 1) * own, :] = (
                moved[:feats, lanes].astype(jnp.bfloat16).reshape(parts, own, LANES)
            )
            sides.append(moved[feats : feats + 3, lanes])
    packed = jnp.concatenate(
        [sides[c][i : i + 1] for i in range(3) for c in range(chunks)], axis=0
    ).astype(jnp.bfloat16)
    for d in range(parts):
        sent_ref[d, chunks * own :, :] = packed


def search_tables(edges):
    feats = edges.shape[0]
    lane = iota((feats, LANES), 1)
    low, high = edges[:, :LANES], edges[:, LANES:]

    def pick(index):
        place = jnp.where(index >= LANES, index - LANES, index)
        return jnp.where(
            index >= LANES,
            look_up(high, place),
            look_up(low, place),
        )

    inner = jnp.zeros((feats, LANES), jnp.int32)
    for level in range(7):
        start = 1 << level
        inner = jnp.where(lane >= start, (2 * (lane - start) + 1) * (1 << (7 - level)), inner)
    return pick(inner), pick(2 * lane + 1)


def gain_kernel(
    sent_ref, edge_ref, gain_ref, best_ref,
    side_ref, wide_edge_ref, even_fine_ref, even_coarse_ref, even_side_ref,
    odd_fine_ref, odd_coarse_ref, odd_side_ref,
    stat_ref, wide_ref, hist_ref, total_ref, top_ref,
):
    parts = sent_ref.shape[0]
    feats, bins = edge_ref.shape
    chunks = (sent_ref.shape[1] - 24) // feats
    per_vector = LANES // PIECE
    tile_rows = even_fine_ref.shape[2]
    quads = feats // QUAD

    hist_ref[...] = jnp.zeros_like(hist_ref)
    total = jnp.zeros((16, NODES), jnp.float32)
    for s in range(parts):
        side = sent_ref[s, chunks * feats :, :].astype(jnp.float32)
        side_ref[s] = side
        for c in range(0, chunks, 2):
            grad, hess, node = [
                jnp.concatenate([side[8 * i + c : 8 * i + c + 1], side[8 * i + c + 1 : 8 * i + c + 2]], axis=1)
                for i in range(3)
            ]
            wide = (NODES, 2 * LANES)
            member = jnp.where(
                jnp.broadcast_to(node, wide).astype(jnp.bfloat16)
                == iota(wide, 0).astype(jnp.float32).astype(jnp.bfloat16),
                jnp.bfloat16(1),
                jnp.bfloat16(0),
            )
            both = jnp.concatenate(
                [jnp.broadcast_to(grad, (8, 2 * LANES)), jnp.broadcast_to(hess, (8, 2 * LANES))], axis=0
            ).astype(jnp.bfloat16)
            total = total + dot_nt(both, member)
    spread = jnp.concatenate([total, jnp.zeros((16, LANES - NODES), jnp.float32)], axis=1)
    for n in range(NODES):
        total_ref[n] = jnp.broadcast_to(spread[:, n : n + 1], (16, LANES))

    edges = edge_ref[...]
    inner, leaf = search_tables(edges)

    for j in range(8):
        wide_edge_ref[j] = jnp.broadcast_to(edges[:, 32 * j : 32 * j + 1], (feats, LANES))

    def search(value):
        bits = []
        for level in range(3):
            choice = [wide_edge_ref[(2 * m + 1) << (2 - level)] for m in range(1 << level)]
            for bit in reversed(bits):
                choice = [
                    jnp.where(bit, choice[2 * m + 1], choice[2 * m])
                    for m in range(len(choice) // 2)
                ]
            bits.append(value >= choice[0])
        place = jnp.where(bits[0], 12, 8)
        for level in range(1, 3):
            place = place + jnp.where(bits[level], 4 >> level, 0)
        for level in range(3, 8):
            if level < 7:
                edge = look_up(inner, place)
            else:
                edge = look_up(leaf, place - LANES)
            place = place + place + jnp.where(value >= edge, 1, 0)
        return jnp.where(value >= wide_edge_ref[0], place - 256, -1)

    def shuffle(pieces, block):
        pieces = list(pieces)
        step = per_vector // 2
        while step >= 1:
            keep = (block & step) == 0
            for s in range(per_vector):
                if s & step == 0:
                    a, b = pieces[s], pieces[s + step]
                    pieces[s] = jnp.where(keep, a, pltpu.roll(b, step * PIECE, 1))
                    pieces[s + step] = jnp.where(keep, pltpu.roll(a, LANES - step * PIECE, 1), b)
            step //= 2
        return pieces

    block = iota((feats, LANES), 1) // PIECE
    block_side = iota((3, LANES), 1) // PIECE

    def prepare(c, fine_ref, coarse_ref, side_tile_ref):
        least, most = [None] * per_vector, [None] * per_vector
        for q in range(parts // per_vector):
            slots, sides = [], []
            for s in range(q * per_vector, (q + 1) * per_vector):
                value = sent_ref[s, pl.ds(pl.multiple_of(c * feats, feats), feats), :]
                slots.append(search(value.astype(jnp.float32)))
                sides.append(side_ref[s, pl.ds(c, 3, stride=8), :])
            lanes = slice(q * LANES, (q + 1) * LANES)
            for j, slot in enumerate(shuffle(slots, block)):
                coarse_ref[j, :, lanes] = (slot >> 5).astype(jnp.float32)
                fine_ref[j, :, lanes] = (slot & 31).astype(jnp.float32)
            for j, side in enumerate(shuffle(sides, block_side)):
                side_tile_ref[j, 0:3, lanes] = side
                node = side[2:3]
                least[j] = node if q == 0 else jnp.minimum(least[j], node)
                most[j] = node if q == 0 else jnp.maximum(most[j], node)
        return [
            (
                jnp.minimum(jnp.min(least[j]).astype(jnp.int32), NODES - NODE_BLOCK),
                jnp.max(most[j]).astype(jnp.int32),
            )
            for j in range(per_vector)
        ]

    fine_index = iota((FINE, tile_rows), 0).astype(jnp.float32).astype(jnp.bfloat16)
    coarse_index = (iota((2 * COARSE, tile_rows), 0) & (COARSE - 1)).astype(jnp.float32)
    coarse_index = coarse_index.astype(jnp.bfloat16)
    is_grad = iota((2 * COARSE, tile_rows), 0) < COARSE
    quarter = iota((2 * COARSE, LANES), 1) // FINE
    zero = jnp.bfloat16(0)
    one = jnp.bfloat16(1)
    deep = 2 * COARSE

    def mask_nodes(first, count, node_wide, both):
        return [
            jnp.where(node_wide == (first + b).astype(jnp.float32).astype(jnp.bfloat16), both, zero)
            for b in range(count)
        ]

    def add_product(u, q, first, masked):
        here = [wide_ref[u, q * QUAD + i] for i in range(QUAD)]
        stream = jnp.concatenate([here[i] * m for m in masked for i in range(QUAD)], axis=0)
        product = dot_nt(stream, stat_ref[u, q])
        for b in range(len(masked)):
            at = b * QUAD * deep
            packed = product[at : at + deep]
            for i in range(1, QUAD):
                packed = jnp.where(
                    quarter == i, product[at + deep * i : at + deep * (i + 1)], packed
                )
            hist_ref[first + b, q] += packed

    def tile_sides(side_tile_ref, u):
        wide = (deep, tile_rows)
        both = jnp.where(
            is_grad,
            jnp.broadcast_to(side_tile_ref[u, 0:1, :], wide),
            jnp.broadcast_to(side_tile_ref[u, 1:2, :], wide),
        ).astype(jnp.bfloat16)
        node = side_tile_ref[u, 2:3, :]
        return node, jnp.broadcast_to(node, wide).astype(jnp.bfloat16), both

    def accumulate(ranges, fine_ref, coarse_ref, side_tile_ref):
        for u in range(per_vector):
            node, node_wide, both = tile_sides(side_tile_ref, u)
            masked = mask_nodes(ranges[u][0], NODE_BLOCK, node_wide, both)
            for q in range(quads):
                for i in range(QUAD):
                    f = q * QUAD + i
                    fine = jnp.broadcast_to(fine_ref[u, f : f + 1, :], (FINE, tile_rows))
                    stat_ref[u, q, i * FINE : (i + 1) * FINE, :] = jnp.where(
                        fine.astype(jnp.bfloat16) <= fine_index, one, zero
                    )
                    coarse = jnp.broadcast_to(coarse_ref[u, f : f + 1, :], (deep, tile_rows))
                    wide_ref[u, f] = jnp.where(
                        coarse.astype(jnp.bfloat16) == coarse_index, one, zero
                    )
                add_product(u, q, ranges[u][0], masked)

    def accumulate_rest(ranges, side_tile_ref):
        for u in range(per_vector):
            first, last = ranges[u]

            @pl.loop(first + NODE_BLOCK, last + 1)
            def _(n):
                node, node_wide, both = tile_sides(side_tile_ref, u)
                masked = mask_nodes(n, 1, node_wide, both)
                for q in range(quads):
                    add_product(u, q, n, masked)

    even = (even_fine_ref, even_coarse_ref, even_side_ref)
    odd = (odd_fine_ref, odd_coarse_ref, odd_side_ref)

    def two_chunks(pair, ranges):
        accumulate(ranges, *even)
        later = prepare(2 * pair + 1, *odd)
        accumulate_rest(ranges, even_side_ref)
        accumulate(later, *odd)
        following = prepare(jnp.minimum(2 * pair + 2, chunks - 1), *even)
        accumulate_rest(later, odd_side_ref)
        return following

    lax.fori_loop(0, chunks // 2, two_chunks, prepare(0, *even))

    row = iota((COARSE, LANES), 0)
    last_lane = iota((COARSE, LANES), 1) | (FINE - 1)

    def left_sums(part):
        ends = look_up(part, last_lane)
        shift = 1
        while shift < COARSE:
            ends = ends + jnp.where(row >= shift, pltpu.roll(ends, shift, 0), 0.0)
            shift *= 2
        return part + jnp.where(row >= 1, pltpu.roll(ends, 1, 0), 0.0)

    @pl.loop(0, NODES // 4)
    def _(group):
        for k in range(4):
            n = 4 * group + k
            grad_total = total_ref[n, :COARSE]
            hess_total = total_ref[n, COARSE:]
            whole = jnp.square(grad_total) / (hess_total + PENALTY)
            for q in range(quads):
                part = hist_ref[n, q]
                grad_left = left_sums(part[:COARSE])
                hess_left = left_sums(part[COARSE:])
                split = jnp.square(grad_left) / (hess_left + PENALTY)
                split = split + jnp.square(grad_total - grad_left) / (
                    hess_total - hess_left + PENALTY
                )
                split = split - whole
                top_ref[q, pl.ds(n, 1), :] = jnp.max(split, axis=0, keepdims=True)

    best = None
    for q in range(quads):
        top = top_ref[q]
        shift = FINE // 2
        while shift >= 1:
            top = jnp.maximum(top, pltpu.roll(top, LANES - shift, 1))
            shift //= 2
        turned = top.T
        for i in range(QUAD):
            found = turned[FINE * i : FINE * i + 1]
            gain_ref[QUAD * q + i : QUAD * q + i + 1] = found
            best = found if best is None else jnp.maximum(best, found)
    best_ref[...] = jnp.broadcast_to(best, best_ref.shape)


def on_device(features, cut_points, grad, hess, node_ids):
    parts = lax.axis_size("row")
    others = parts * lax.axis_size("feat")
    rows, feats = features.shape
    own = feats // parts
    bins = cut_points.shape[1]
    length = (own + 3) * rows // LANES
    in_vmem = pl.BlockSpec(memory_space=pltpu.VMEM)
    sent = pl.pallas_call(
        sort_kernel,
        out_shape=jax.ShapeDtypeStruct((parts, length, LANES), jnp.bfloat16),
        in_specs=[pl.BlockSpec(memory_space=pltpu.MemorySpace.HBM)] * 4,
        out_specs=in_vmem,
        scratch_shapes=[
            pltpu.VMEM((rows, feats), jnp.bfloat16),
            pltpu.VMEM((1, rows), jnp.float32),
            pltpu.VMEM((1, rows), jnp.float32),
            pltpu.VMEM((1, rows), jnp.int32),
            pltpu.SemaphoreType.DMA((4,)),
        ],
        name="sort_rows",
        compiler_params=pltpu.CompilerParams(vmem_limit_bytes=67043328),
    )(features, grad[None], hess[None], node_ids[None])
    gathered = lax.all_to_all(sent, "row", 0, 0)
    edges = lax.dynamic_slice_in_dim(cut_points, lax.axis_index("row") * own, own, 0)
    tile_rows = PIECE * parts
    feature_gain, best = pl.pallas_call(
        gain_kernel,
        out_shape=(
            jax.ShapeDtypeStruct((own, NODES), jnp.float32),
            jax.ShapeDtypeStruct((others, NODES), jnp.float32),
        ),
        in_specs=[in_vmem] * 2,
        out_specs=(in_vmem, in_vmem),
        scratch_shapes=[
            pltpu.VMEM((parts, 24, LANES), jnp.float32),
            pltpu.VMEM((8, own, LANES), jnp.float32),
            *[
                pltpu.VMEM((LANES // PIECE, height, tile_rows), jnp.float32)
                for height in (own, own, 8, own, own, 8)
            ],
            pltpu.VMEM((LANES // PIECE, own // QUAD, QUAD * FINE, tile_rows), jnp.bfloat16),
            pltpu.VMEM((LANES // PIECE, own, 2 * COARSE, tile_rows), jnp.bfloat16),
            pltpu.VMEM((NODES, own // QUAD, 2 * COARSE, LANES), jnp.float32),
            pltpu.VMEM((NODES, 2 * COARSE, LANES), jnp.float32),
            pltpu.VMEM((own // QUAD, NODES, LANES), jnp.float32),
        ],
        name="split_gain",
        compiler_params=pltpu.CompilerParams(vmem_limit_bytes=40 << 20),
    )(gathered, edges)
    node_best = jnp.max(lax.all_to_all(best, ("row", "feat"), 0, 0), axis=0)
    return (feature_gain, node_best)


def solution(mesh):
    placed = (P("row", "feat"), P("feat", None), P("row"), P("row"), P("row"))
    return jax.shard_map(
        on_device,
        mesh=mesh,
        in_specs=placed,
        out_specs=(P(("feat", "row"), None), P()),
        check_vma=False,
    )
```

```python
import jax
import jax.numpy as jnp
from jax import lax
from jax.experimental import pallas as pl
from jax.experimental.pallas import tpu as pltpu
from jax.sharding import PartitionSpec as P

NODES = 32
PENALTY = 1.0
LANES = 128
COARSE = 8
FINE = 32
PIECE = 32
QUAD = 4
NODE_BLOCK = 4
PAIRED = 1


def dot_nt(left, right):
    return lax.dot_general(
        left, right, (((1,), (1,)), ((), ())), preferred_element_type=jnp.float32
    )


def iota(shape, axis):
    return lax.broadcasted_iota(jnp.int32, shape, axis)


def look_up(table, index):
    return jnp.take_along_axis(table, index, axis=1, mode="promise_in_bounds")


def sort_kernel(
    value_in, grad_in, hess_in, node_in, sent_ref, value_ref, grad_ref, hess_ref, node_ref, arrived
):
    pairs = ((node_in, node_ref), (grad_in, grad_ref), (hess_in, hess_ref), (value_in, value_ref))
    copies = [
        pltpu.make_async_copy(source, target, arrived.at[k])
        for k, (source, target) in enumerate(pairs)
    ]
    for copy in copies:
        copy.start()
    rows, feats = value_ref.shape
    parts = sent_ref.shape[0]
    own = feats // parts
    chunks = rows // LANES
    copies[0].wait()
    node = node_ref[...]
    member = (jnp.broadcast_to(node, (NODES, rows)) == iota((NODES, rows), 0)).astype(jnp.float32)
    earlier = (jnp.broadcast_to(node, (NODES, rows)) < iota((NODES, rows), 0)).astype(jnp.float32)
    upper = (iota((LANES, LANES), 0) <= iota((LANES, LANES), 1)).astype(jnp.bfloat16)
    offset = jnp.sum(earlier, axis=1, keepdims=True)
    ranks = []
    for c in range(chunks):
        piece = member[:, c * LANES : (c + 1) * LANES]
        running = jnp.dot(piece.astype(jnp.bfloat16), upper, preferred_element_type=jnp.float32)
        ranks.append(jnp.sum(piece * (running + (offset - 1.0)), axis=0, keepdims=True))
        offset = offset + jnp.sum(piece, axis=1, keepdims=True)
    rank = jnp.concatenate(ranks, axis=1).astype(jnp.int32)

    for copy in copies[1:]:
        copy.wait()
    side = jnp.concatenate(
        [grad_ref[...], hess_ref[...], node.astype(jnp.float32), jnp.zeros((13, rows), jnp.float32)],
        axis=0,
    ).astype(jnp.bfloat16)
    operand = jnp.concatenate([value_ref[...].T, side], axis=0)
    block = 2 * LANES
    sides = []
    for b in range(rows // block):
        chosen = jnp.where(
            jnp.broadcast_to(rank, (block, rows)) == iota((block, rows), 0) + b * block, 1.0, 0.0
        ).astype(jnp.bfloat16)
        moved = dot_nt(operand, chosen)
        for half in range(2):
            c = 2 * b + half
            lanes = slice(half * LANES, (half + 1) * LANES)
            sent_ref[:, c * own : (c + 1) * own, :] = (
                moved[:feats, lanes].astype(jnp.bfloat16).reshape(parts, own, LANES)
            )
            sides.append(moved[feats : feats + 3, lanes])
    packed = jnp.concatenate(
        [sides[c][i : i + 1] for i in range(3) for c in range(chunks)], axis=0
    ).astype(jnp.bfloat16)
    for d in range(parts):
        sent_ref[d, chunks * own :, :] = packed


def search_tables(edges):
    feats = edges.shape[0]
    lane = iota((feats, LANES), 1)
    low, high = edges[:, :LANES], edges[:, LANES:]

    def pick(index):
        place = jnp.where(index >= LANES, index - LANES, index)
        return jnp.where(
            index >= LANES,
            look_up(high, place),
            look_up(low, place),
        )

    inner = jnp.zeros((feats, LANES), jnp.int32)
    for level in range(7):
        start = 1 << level
        inner = jnp.where(lane >= start, (2 * (lane - start) + 1) * (1 << (7 - level)), inner)
    return pick(inner), pick(2 * lane + 1)


def gain_kernel(
    sent_ref, edge_ref, gain_ref, best_ref,
    side_ref, wide_edge_ref, even_fine_ref, even_coarse_ref, even_side_ref,
    odd_fine_ref, odd_coarse_ref, odd_side_ref,
    stat_ref, paired_ref, wide_ref, hist_ref, total_ref, top_ref,
):
    parts = sent_ref.shape[0]
    feats, bins = edge_ref.shape
    chunks = (sent_ref.shape[1] - 24) // feats
    per_vector = LANES // PIECE
    tile_rows = even_fine_ref.shape[2]
    quads = feats // QUAD

    hist_ref[...] = jnp.zeros_like(hist_ref)
    total = jnp.zeros((16, NODES), jnp.float32)
    for s in range(parts):
        side = sent_ref[s, chunks * feats :, :].astype(jnp.float32)
        side_ref[s] = side
        for c in range(0, chunks, 2):
            grad, hess, node = [
                jnp.concatenate([side[8 * i + c : 8 * i + c + 1], side[8 * i + c + 1 : 8 * i + c + 2]], axis=1)
                for i in range(3)
            ]
            wide = (NODES, 2 * LANES)
            member = jnp.where(
                jnp.broadcast_to(node, wide).astype(jnp.bfloat16)
                == iota(wide, 0).astype(jnp.float32).astype(jnp.bfloat16),
                jnp.bfloat16(1),
                jnp.bfloat16(0),
            )
            both = jnp.concatenate(
                [jnp.broadcast_to(grad, (8, 2 * LANES)), jnp.broadcast_to(hess, (8, 2 * LANES))], axis=0
            ).astype(jnp.bfloat16)
            total = total + dot_nt(both, member)
    spread = jnp.concatenate([total, jnp.zeros((16, LANES - NODES), jnp.float32)], axis=1)
    for n in range(NODES):
        total_ref[n] = jnp.broadcast_to(spread[:, n : n + 1], (16, LANES))

    edges = edge_ref[...]
    inner, leaf = search_tables(edges)

    for j in range(8):
        wide_edge_ref[j] = jnp.broadcast_to(edges[:, 32 * j : 32 * j + 1], (feats, LANES))

    def search(value):
        bits = []
        for level in range(3):
            choice = [wide_edge_ref[(2 * m + 1) << (2 - level)] for m in range(1 << level)]
            for bit in reversed(bits):
                choice = [
                    jnp.where(bit, choice[2 * m + 1], choice[2 * m])
                    for m in range(len(choice) // 2)
                ]
            bits.append(value >= choice[0])
        place = jnp.where(bits[0], 12, 8)
        for level in range(1, 3):
            place = place + jnp.where(bits[level], 4 >> level, 0)
        for level in range(3, 8):
            if level < 7:
                edge = look_up(inner, place)
            else:
                edge = look_up(leaf, place - LANES)
            place = place + place + jnp.where(value >= edge, 1, 0)
        return jnp.where(value >= wide_edge_ref[0], place - 256, -1)

    def shuffle(pieces, block):
        pieces = list(pieces)
        step = per_vector // 2
        while step >= 1:
            keep = (block & step) == 0
            for s in range(per_vector):
                if s & step == 0:
                    a, b = pieces[s], pieces[s + step]
                    pieces[s] = jnp.where(keep, a, pltpu.roll(b, step * PIECE, 1))
                    pieces[s + step] = jnp.where(keep, pltpu.roll(a, LANES - step * PIECE, 1), b)
            step //= 2
        return pieces

    block = iota((feats, LANES), 1) // PIECE
    block_side = iota((3, LANES), 1) // PIECE

    def prepare(c, fine_ref, coarse_ref, side_tile_ref):
        least, most = [None] * per_vector, [None] * per_vector
        for q in range(parts // per_vector):
            slots, sides = [], []
            for s in range(q * per_vector, (q + 1) * per_vector):
                value = sent_ref[s, pl.ds(pl.multiple_of(c * feats, feats), feats), :]
                slots.append(search(value.astype(jnp.float32)))
                sides.append(side_ref[s, pl.ds(c, 3, stride=8), :])
            lanes = slice(q * LANES, (q + 1) * LANES)
            for j, slot in enumerate(shuffle(slots, block)):
                coarse_ref[j, :, lanes] = (slot >> 5).astype(jnp.float32)
                fine_ref[j, :, lanes] = (slot & 31).astype(jnp.float32)
            for j, side in enumerate(shuffle(sides, block_side)):
                side_tile_ref[j, 0:3, lanes] = side
                node = side[2:3]
                least[j] = node if q == 0 else jnp.minimum(least[j], node)
                most[j] = node if q == 0 else jnp.maximum(most[j], node)
        return [
            (
                jnp.minimum(jnp.min(least[j]).astype(jnp.int32), NODES - NODE_BLOCK),
                jnp.max(most[j]).astype(jnp.int32),
            )
            for j in range(per_vector)
        ]

    deep = 2 * COARSE
    pair_rows = (deep, tile_rows)
    step_index = (iota(pair_rows, 0) & 7).astype(jnp.float32)
    fine_index = [(step_index + 8.0 * j).astype(jnp.bfloat16) for j in range(FINE // 8)]
    coarse_index = step_index.astype(jnp.bfloat16)
    quarter_lane = iota((COARSE, LANES), 1)
    quarter = ((quarter_lane >> 6) << 1) | ((quarter_lane >> 3) & 1)
    zero = jnp.bfloat16(0)
    one = jnp.bfloat16(1)
    two = jnp.bfloat16(2)

    def mask_nodes(first, count, node_wide, both):
        return [
            jnp.where(node_wide == (first + b).astype(jnp.float32).astype(jnp.bfloat16), part, zero)
            for b in range(count)
            for part in both
        ]

    def add_product(u, q, first, masked):
        here = [wide_ref[u, q * (QUAD // 2) + i] for i in range(QUAD // 2)]
        stream = jnp.concatenate([h * m for m in masked for h in here], axis=0)
        product = dot_nt(stream, stat_ref[u, q])
        for k in range(len(masked)):
            add_block(first + k // 2, q, k % 2, product[k * 32 : k * 32 + 32])

    def add_block(n, q, k, part):
        packed = part[:COARSE]
        for i in range(1, QUAD):
            packed = jnp.where(quarter == i, part[COARSE * i : COARSE * (i + 1)], packed)
        hist_ref[n, q, k * COARSE : (k + 1) * COARSE] += packed

    def add_paired(u, q, first, masked):
        here = [wide_ref[u, q * (QUAD // 2) + i] for i in range(QUAD // 2)]
        stream = jnp.concatenate([h * m for m in masked for h in here], axis=0)
        product = dot_nt(stream, paired_ref[u, q - (quads - PAIRED)])
        for k in range(len(masked)):
            for odd in range(2):
                add_block(
                    first + 2 * (k // 2) + odd, q, k % 2,
                    product[k * 32 : k * 32 + 32, odd * LANES : (odd + 1) * LANES],
                )

    def tile_sides(side_tile_ref, u):
        grad, hess, node = [
            jnp.broadcast_to(side_tile_ref[u, k : k + 1, :], pair_rows).astype(jnp.bfloat16)
            for k in range(3)
        ]
        return node, (grad, hess)

    def pair_of(ref, u, f):
        return jnp.concatenate(
            [
                jnp.broadcast_to(ref[u, f + k : f + k + 1, :], (COARSE, tile_rows))
                for k in range(2)
            ],
            axis=0,
        ).astype(jnp.bfloat16)

    def accumulate(ranges, fine_ref, coarse_ref, side_tile_ref):
        for u in range(per_vector):
            node_wide, both = tile_sides(side_tile_ref, u)
            first = ranges[u][0]
            masked = mask_nodes(first, NODE_BLOCK, node_wide, both)
            place = node_wide - first.astype(jnp.float32).astype(jnp.bfloat16)
            second = place >= two
            coupled = [jnp.where(second, zero, part) for part in both] + [
                jnp.where(second, part, zero) for part in both
            ]
            parity = [
                jnp.where(place == jnp.bfloat16(k), one, jnp.where(place == jnp.bfloat16(k + 2), one, zero))
                for k in range(2)
            ]
            for q in range(quads):
                for i in range(QUAD // 2):
                    f = q * QUAD + 2 * i
                    fine = pair_of(fine_ref, u, f)
                    for j in range(FINE // 8):
                        at = i * 2 * FINE + deep * j
                        inside = fine <= fine_index[j]
                        if q < quads - PAIRED:
                            stat_ref[u, q, at : at + deep, :] = jnp.where(inside, one, zero)
                        else:
                            for k in range(2):
                                low = k * LANES + at
                                paired_ref[u, q - (quads - PAIRED), low : low + deep, :] = (
                                    jnp.where(inside, parity[k], zero)
                                )
                    coarse = pair_of(coarse_ref, u, f)
                    wide_ref[u, f // 2] = jnp.where(coarse == coarse_index, one, zero)
                if q < quads - PAIRED:
                    add_product(u, q, first, masked)
                else:
                    add_paired(u, q, first, coupled)

    def accumulate_rest(ranges, fine_ref, side_tile_ref):
        for u in range(per_vector):
            first, last = ranges[u]

            @pl.loop(first + NODE_BLOCK, last + 1)
            def _(n):
                node_wide, both = tile_sides(side_tile_ref, u)
                masked = mask_nodes(n, 1, node_wide, both)
                for q in range(quads):
                    if q >= quads - PAIRED:
                        for i in range(QUAD // 2):
                            fine = pair_of(fine_ref, u, q * QUAD + 2 * i)
                            for j in range(FINE // 8):
                                at = i * 2 * FINE + deep * j
                                stat_ref[u, q, at : at + deep, :] = jnp.where(
                                    fine <= fine_index[j], one, zero
                                )
                    add_product(u, q, n, masked)

    even = (even_fine_ref, even_coarse_ref, even_side_ref)
    odd = (odd_fine_ref, odd_coarse_ref, odd_side_ref)

    def two_chunks(pair, ranges):
        accumulate(ranges, *even)
        later = prepare(2 * pair + 1, *odd)
        accumulate_rest(ranges, even_fine_ref, even_side_ref)
        accumulate(later, *odd)
        following = prepare(jnp.minimum(2 * pair + 2, chunks - 1), *even)
        accumulate_rest(later, odd_fine_ref, odd_side_ref)
        return following

    lax.fori_loop(0, chunks // 2, two_chunks, prepare(0, *even))

    row = iota((COARSE, LANES), 0)
    last_lane = iota((COARSE, LANES), 1) | 55

    def left_sums(part):
        ends = look_up(part, last_lane)
        shift = 1
        while shift < COARSE:
            ends = ends + jnp.where(row >= shift, pltpu.roll(ends, shift, 0), 0.0)
            shift *= 2
        return part + jnp.where(row >= 1, pltpu.roll(ends, 1, 0), 0.0)

    @pl.loop(0, NODES // 4)
    def _(group):
        for k in range(4):
            n = 4 * group + k
            grad_total = total_ref[n, :COARSE]
            hess_total = total_ref[n, COARSE:]
            whole = jnp.square(grad_total) / (hess_total + PENALTY)
            for q in range(quads):
                part = hist_ref[n, q]
                grad_left = left_sums(part[:COARSE])
                hess_left = left_sums(part[COARSE:])
                split = jnp.square(grad_left) / (hess_left + PENALTY)
                split = split + jnp.square(grad_total - grad_left) / (
                    hess_total - hess_left + PENALTY
                )
                split = split - whole
                top_ref[q, pl.ds(n, 1), :] = jnp.max(split, axis=0, keepdims=True)

    best = None
    for q in range(quads):
        top = top_ref[q]
        for shift in (32, 16, 4, 2, 1):
            top = jnp.maximum(top, pltpu.roll(top, LANES - shift, 1))
        turned = top.T
        for i in range(QUAD):
            found = turned[64 * (i // 2) + 8 * (i % 2) : 64 * (i // 2) + 8 * (i % 2) + 1]
            gain_ref[QUAD * q + i : QUAD * q + i + 1] = found
            best = found if best is None else jnp.maximum(best, found)
    best_ref[...] = jnp.broadcast_to(best, best_ref.shape)


def on_device(features, cut_points, grad, hess, node_ids):
    parts = lax.axis_size("row")
    others = parts * lax.axis_size("feat")
    rows, feats = features.shape
    own = feats // parts
    bins = cut_points.shape[1]
    length = (own + 3) * rows // LANES
    in_vmem = pl.BlockSpec(memory_space=pltpu.VMEM)
    sent = pl.pallas_call(
        sort_kernel,
        out_shape=jax.ShapeDtypeStruct((parts, length, LANES), jnp.bfloat16),
        in_specs=[pl.BlockSpec(memory_space=pltpu.MemorySpace.HBM)] * 4,
        out_specs=in_vmem,
        scratch_shapes=[
            pltpu.VMEM((rows, feats), jnp.bfloat16),
            pltpu.VMEM((1, rows), jnp.float32),
            pltpu.VMEM((1, rows), jnp.float32),
            pltpu.VMEM((1, rows), jnp.int32),
            pltpu.SemaphoreType.DMA((4,)),
        ],
        name="sort_rows",
        compiler_params=pltpu.CompilerParams(vmem_limit_bytes=67043328),
    )(features, grad[None], hess[None], node_ids[None])
    gathered = lax.all_to_all(sent, "row", 0, 0)
    edges = lax.dynamic_slice_in_dim(cut_points, lax.axis_index("row") * own, own, 0)
    tile_rows = PIECE * parts
    feature_gain, best = pl.pallas_call(
        gain_kernel,
        out_shape=(
            jax.ShapeDtypeStruct((own, NODES), jnp.float32),
            jax.ShapeDtypeStruct((others, NODES), jnp.float32),
        ),
        in_specs=[in_vmem] * 2,
        out_specs=(in_vmem, in_vmem),
        scratch_shapes=[
            pltpu.VMEM((parts, 24, LANES), jnp.float32),
            pltpu.VMEM((8, own, LANES), jnp.float32),
            *[
                pltpu.VMEM((LANES // PIECE, height, tile_rows), jnp.float32)
                for height in (own, own, 8, own, own, 8)
            ],
            pltpu.VMEM((LANES // PIECE, own // QUAD, QUAD * FINE, tile_rows), jnp.bfloat16),
            pltpu.VMEM((LANES // PIECE, PAIRED, 2 * QUAD * FINE, tile_rows), jnp.bfloat16),
            pltpu.VMEM((LANES // PIECE, own // 2, 2 * COARSE, tile_rows), jnp.bfloat16),
            pltpu.VMEM((NODES, own // QUAD, 2 * COARSE, LANES), jnp.float32),
            pltpu.VMEM((NODES, 2 * COARSE, LANES), jnp.float32),
            pltpu.VMEM((own // QUAD, NODES, LANES), jnp.float32),
        ],
        name="split_gain",
        compiler_params=pltpu.CompilerParams(vmem_limit_bytes=40 << 20),
    )(gathered, edges)
    node_best = jnp.max(lax.all_to_all(best, ("row", "feat"), 0, 0), axis=0)
    return (feature_gain, node_best)


def solution(mesh):
    placed = (P("row", "feat"), P("feat", None), P("row"), P("row"), P("row"))
    return jax.shard_map(
        on_device,
        mesh=mesh,
        in_specs=placed,
        out_specs=(P(("feat", "row"), None), P()),
        check_vma=False,
    )
```

```python
import jax
import jax.numpy as jnp
from jax import lax
from jax.experimental import pallas as pl
from jax.experimental.pallas import tpu as pltpu
from jax.sharding import PartitionSpec as P

NODES = 32
PENALTY = 1.0
LANES = 128
COARSE = 8
FINE = 32
PIECE = 32
QUAD = 4
NODE_BLOCK = 4
PAIRED = 1


def dot_nt(left, right):
    return lax.dot_general(
        left, right, (((1,), (1,)), ((), ())), preferred_element_type=jnp.float32
    )


def iota(shape, axis):
    return lax.broadcasted_iota(jnp.int32, shape, axis)


def look_up(table, index):
    return jnp.take_along_axis(table, index, axis=1, mode="promise_in_bounds")


def sort_kernel(
    value_in, grad_in, hess_in, node_in, sent_ref, value_ref, grad_ref, hess_ref, node_ref, arrived
):
    pairs = ((node_in, node_ref), (grad_in, grad_ref), (hess_in, hess_ref), (value_in, value_ref))
    copies = [
        pltpu.make_async_copy(source, target, arrived.at[k])
        for k, (source, target) in enumerate(pairs)
    ]
    for copy in copies:
        copy.start()
    rows, feats = value_ref.shape
    parts = sent_ref.shape[0]
    own = feats // parts
    chunks = rows // LANES
    copies[0].wait()
    node = node_ref[...]
    member = (jnp.broadcast_to(node, (NODES, rows)) == iota((NODES, rows), 0)).astype(jnp.float32)
    earlier = (jnp.broadcast_to(node, (NODES, rows)) < iota((NODES, rows), 0)).astype(jnp.float32)
    upper = (iota((LANES, LANES), 0) <= iota((LANES, LANES), 1)).astype(jnp.bfloat16)
    offset = jnp.sum(earlier, axis=1, keepdims=True)
    ranks = []
    for c in range(chunks):
        piece = member[:, c * LANES : (c + 1) * LANES]
        running = jnp.dot(piece.astype(jnp.bfloat16), upper, preferred_element_type=jnp.float32)
        ranks.append(jnp.sum(piece * (running + (offset - 1.0)), axis=0, keepdims=True))
        offset = offset + jnp.sum(piece, axis=1, keepdims=True)
    rank = jnp.concatenate(ranks, axis=1).astype(jnp.int32)

    for copy in copies[1:]:
        copy.wait()
    side = jnp.concatenate(
        [grad_ref[...], hess_ref[...], node.astype(jnp.float32), jnp.zeros((13, rows), jnp.float32)],
        axis=0,
    ).astype(jnp.bfloat16)
    operand = jnp.concatenate([value_ref[...].T, side], axis=0)
    block = 2 * LANES
    sides = []
    for b in range(rows // block):
        chosen = jnp.where(
            jnp.broadcast_to(rank, (block, rows)) == iota((block, rows), 0) + b * block, 1.0, 0.0
        ).astype(jnp.bfloat16)
        moved = dot_nt(operand, chosen)
        for half in range(2):
            c = 2 * b + half
            lanes = slice(half * LANES, (half + 1) * LANES)
            sent_ref[:, c * own : (c + 1) * own, :] = (
                moved[:feats, lanes].astype(jnp.bfloat16).reshape(parts, own, LANES)
            )
            sides.append(moved[feats : feats + 3, lanes])
    packed = jnp.concatenate(
        [sides[c][i : i + 1] for i in range(3) for c in range(chunks)], axis=0
    ).astype(jnp.bfloat16)
    for d in range(parts):
        sent_ref[d, chunks * own :, :] = packed


def search_tables(edges):
    feats = edges.shape[0]
    lane = iota((feats, LANES), 1)
    low, high = edges[:, :LANES], edges[:, LANES:]

    def pick(index):
        place = jnp.where(index >= LANES, index - LANES, index)
        return jnp.where(
            index >= LANES,
            look_up(high, place),
            look_up(low, place),
        )

    inner = jnp.zeros((feats, LANES), jnp.int32)
    for level in range(7):
        start = 1 << level
        inner = jnp.where(lane >= start, (2 * (lane - start) + 1) * (1 << (7 - level)), inner)
    return pick(inner), pick(2 * lane + 1)


def gain_kernel(
    sent_ref, edge_ref, gain_ref, best_ref,
    side_ref, wide_edge_ref, even_fine_ref, even_coarse_ref, even_side_ref,
    odd_fine_ref, odd_coarse_ref, odd_side_ref,
    stat_ref, paired_ref, wide_ref, hist_ref, total_ref, top_ref,
):
    parts = sent_ref.shape[0]
    feats, bins = edge_ref.shape
    chunks = (sent_ref.shape[1] - 24) // feats
    per_vector = LANES // PIECE
    tile_rows = even_fine_ref.shape[2]
    quads = feats // QUAD

    hist_ref[...] = jnp.zeros_like(hist_ref)
    total = jnp.zeros((16, NODES), jnp.float32)
    for s in range(parts):
        side = sent_ref[s, chunks * feats :, :].astype(jnp.float32)
        side_ref[s] = side
        for c in range(0, chunks, 2):
            grad, hess, node = [
                jnp.concatenate([side[8 * i + c : 8 * i + c + 1], side[8 * i + c + 1 : 8 * i + c + 2]], axis=1)
                for i in range(3)
            ]
            wide = (NODES, 2 * LANES)
            member = jnp.where(
                jnp.broadcast_to(node, wide).astype(jnp.bfloat16)
                == iota(wide, 0).astype(jnp.float32).astype(jnp.bfloat16),
                jnp.bfloat16(1),
                jnp.bfloat16(0),
            )
            both = jnp.concatenate(
                [jnp.broadcast_to(grad, (8, 2 * LANES)), jnp.broadcast_to(hess, (8, 2 * LANES))], axis=0
            ).astype(jnp.bfloat16)
            total = total + dot_nt(both, member)
    spread = jnp.concatenate([total, jnp.zeros((16, LANES - NODES), jnp.float32)], axis=1)
    for n in range(NODES):
        total_ref[n] = jnp.broadcast_to(spread[:, n : n + 1], (16, LANES))

    edges = edge_ref[...]
    inner, leaf = search_tables(edges)

    for j in range(8):
        wide_edge_ref[j] = jnp.broadcast_to(edges[:, 32 * j : 32 * j + 1], (feats, LANES))

    def search(value):
        bits = []
        for level in range(3):
            choice = [wide_edge_ref[(2 * m + 1) << (2 - level)] for m in range(1 << level)]
            for bit in reversed(bits):
                choice = [
                    jnp.where(bit, choice[2 * m + 1], choice[2 * m])
                    for m in range(len(choice) // 2)
                ]
            bits.append(value >= choice[0])
        place = jnp.where(bits[0], 12, 8)
        for level in range(1, 3):
            place = place + jnp.where(bits[level], 4 >> level, 0)
        for level in range(3, 8):
            if level < 7:
                edge = look_up(inner, place)
            else:
                edge = look_up(leaf, place - LANES)
            place = place + place + jnp.where(value >= edge, 1, 0)
        return jnp.where(value >= wide_edge_ref[0], place - 256, -1)

    def shuffle(pieces, block):
        pieces = list(pieces)
        step = per_vector // 2
        while step >= 1:
            keep = (block & step) == 0
            for s in range(per_vector):
                if s & step == 0:
                    a, b = pieces[s], pieces[s + step]
                    pieces[s] = jnp.where(keep, a, pltpu.roll(b, step * PIECE, 1))
                    pieces[s + step] = jnp.where(keep, pltpu.roll(a, LANES - step * PIECE, 1), b)
            step //= 2
        return pieces

    block = iota((feats, LANES), 1) // PIECE
    block_side = iota((3, LANES), 1) // PIECE

    def prepare(c, fine_ref, coarse_ref, side_tile_ref):
        least, most = [None] * per_vector, [None] * per_vector
        for q in range(parts // per_vector):
            slots, sides = [], []
            for s in range(q * per_vector, (q + 1) * per_vector):
                value = sent_ref[s, pl.ds(pl.multiple_of(c * feats, feats), feats), :]
                slots.append(search(value.astype(jnp.float32)))
                sides.append(side_ref[s, pl.ds(c, 3, stride=8), :])
            lanes = slice(q * LANES, (q + 1) * LANES)
            for j, slot in enumerate(shuffle(slots, block)):
                coarse_ref[j, :, lanes] = (slot >> 5).astype(jnp.float32)
                fine_ref[j, :, lanes] = (slot & 31).astype(jnp.float32)
            for j, side in enumerate(shuffle(sides, block_side)):
                side_tile_ref[j, 0:3, lanes] = side
                node = side[2:3]
                least[j] = node if q == 0 else jnp.minimum(least[j], node)
                most[j] = node if q == 0 else jnp.maximum(most[j], node)
        return [
            (
                jnp.minimum(jnp.min(least[j]).astype(jnp.int32), NODES - NODE_BLOCK),
                jnp.max(most[j]).astype(jnp.int32),
            )
            for j in range(per_vector)
        ]

    deep = 2 * COARSE
    pair_rows = (deep, tile_rows)
    step_index = (iota(pair_rows, 0) & 7).astype(jnp.float32)
    fine_index = [(step_index + 8.0 * j).astype(jnp.bfloat16) for j in range(FINE // 8)]
    coarse_index = step_index.astype(jnp.bfloat16)
    quarter_lane = iota((COARSE, LANES), 1)
    quarter = ((quarter_lane >> 6) << 1) | ((quarter_lane >> 3) & 1)
    zero = jnp.bfloat16(0)
    one = jnp.bfloat16(1)
    two = jnp.bfloat16(2)

    def mask_nodes(first, count, node_wide, both):
        return [
            jnp.where(node_wide == (first + b).astype(jnp.float32).astype(jnp.bfloat16), part, zero)
            for b in range(count)
            for part in both
        ]

    def add_product(u, q, first, masked):
        here = [wide_ref[u, q * (QUAD // 2) + i] for i in range(QUAD // 2)]
        stream = jnp.concatenate([h * m for m in masked for h in here], axis=0)
        product = dot_nt(stream, stat_ref[u, q])
        for k in range(len(masked)):
            add_block(first + k // 2, q, k % 2, product[k * 32 : k * 32 + 32])

    def add_block(n, q, k, part):
        packed = part[:COARSE]
        for i in range(1, QUAD):
            packed = jnp.where(quarter == i, part[COARSE * i : COARSE * (i + 1)], packed)
        hist_ref[n, q, k * COARSE : (k + 1) * COARSE] += packed

    def add_paired(u, q, first, masked):
        here = [wide_ref[u, q * (QUAD // 2) + i] for i in range(QUAD // 2)]
        stream = jnp.concatenate([h * m for m in masked for h in here], axis=0)
        product = dot_nt(stream, paired_ref[u, q - (quads - PAIRED)])
        for k in range(len(masked)):
            for odd in range(2):
                add_block(
                    first + 2 * (k // 2) + odd, q, k % 2,
                    product[k * 32 : k * 32 + 32, odd * LANES : (odd + 1) * LANES],
                )

    def tile_sides(side_tile_ref, u):
        grad, hess, node = [
            jnp.broadcast_to(side_tile_ref[u, k : k + 1, :], pair_rows).astype(jnp.bfloat16)
            for k in range(3)
        ]
        return node, (grad, hess)

    def pair_of(ref, u, f):
        return jnp.concatenate(
            [
                jnp.broadcast_to(ref[u, f + k : f + k + 1, :], (COARSE, tile_rows))
                for k in range(2)
            ],
            axis=0,
        ).astype(jnp.bfloat16)

    def accumulate(ranges, fine_ref, coarse_ref, side_tile_ref):
        for u in range(per_vector):
            node_wide, both = tile_sides(side_tile_ref, u)
            first = ranges[u][0]
            masked = mask_nodes(first, NODE_BLOCK, node_wide, both)
            place = node_wide - first.astype(jnp.float32).astype(jnp.bfloat16)
            second = place >= two
            coupled = [jnp.where(second, zero, part) for part in both] + [
                jnp.where(second, part, zero) for part in both
            ]
            parity = [
                jnp.where(place == jnp.bfloat16(k), one, jnp.where(place == jnp.bfloat16(k + 2), one, zero))
                for k in range(2)
            ]
            for q in range(quads):
                for i in range(QUAD // 2):
                    f = q * QUAD + 2 * i
                    fine = pair_of(fine_ref, u, f)
                    for j in range(FINE // 8):
                        at = i * 2 * FINE + deep * j
                        inside = fine <= fine_index[j]
                        if q < quads - PAIRED:
                            stat_ref[u, q, at : at + deep, :] = jnp.where(inside, one, zero)
                        else:
                            for k in range(2):
                                low = k * LANES + at
                                paired_ref[u, q - (quads - PAIRED), low : low + deep, :] = (
                                    jnp.where(inside, parity[k], zero)
                                )
                    coarse = pair_of(coarse_ref, u, f)
                    wide_ref[u, f // 2] = jnp.where(coarse == coarse_index, one, zero)
                if q < quads - PAIRED:
                    add_product(u, q, first, masked)
                else:
                    add_paired(u, q, first, coupled)

    def accumulate_rest(ranges, fine_ref, side_tile_ref):
        for u in range(per_vector):
            first, last = ranges[u]

            @pl.loop(first + NODE_BLOCK, last + 1)
            def _(n):
                node_wide, both = tile_sides(side_tile_ref, u)
                masked = mask_nodes(n, 1, node_wide, both)
                for q in range(quads):
                    if q >= quads - PAIRED:
                        for i in range(QUAD // 2):
                            fine = pair_of(fine_ref, u, q * QUAD + 2 * i)
                            for j in range(FINE // 8):
                                at = i * 2 * FINE + deep * j
                                stat_ref[u, q, at : at + deep, :] = jnp.where(
                                    fine <= fine_index[j], one, zero
                                )
                    add_product(u, q, n, masked)

    even = (even_fine_ref, even_coarse_ref, even_side_ref)
    odd = (odd_fine_ref, odd_coarse_ref, odd_side_ref)

    def two_chunks(pair, ranges):
        accumulate(ranges, *even)
        later = prepare(2 * pair + 1, *odd)
        accumulate_rest(ranges, even_fine_ref, even_side_ref)
        accumulate(later, *odd)
        following = prepare(jnp.minimum(2 * pair + 2, chunks - 1), *even)
        accumulate_rest(later, odd_fine_ref, odd_side_ref)
        return following

    lax.fori_loop(0, chunks // 2, two_chunks, prepare(0, *even))

    row = iota((COARSE, LANES), 0)
    last_lane = iota((COARSE, LANES), 1) | 55

    def left_sums(part):
        ends = look_up(part, last_lane)
        shift = 1
        while shift < COARSE:
            ends = ends + jnp.where(row >= shift, pltpu.roll(ends, shift, 0), 0.0)
            shift *= 2
        return part + jnp.where(row >= 1, pltpu.roll(ends, 1, 0), 0.0)

    @pl.loop(0, NODES // 4)
    def _(group):
        for k in range(4):
            n = 4 * group + k
            grad_total = total_ref[n, :COARSE]
            hess_total = total_ref[n, COARSE:]
            whole = jnp.square(grad_total) / (hess_total + PENALTY)
            for q in range(quads):
                part = hist_ref[n, q]
                grad_left = left_sums(part[:COARSE])
                hess_left = left_sums(part[COARSE:])
                split = jnp.square(grad_left) / (hess_left + PENALTY)
                split = split + jnp.square(grad_total - grad_left) / (
                    hess_total - hess_left + PENALTY
                )
                split = split - whole
                top_ref[q, pl.ds(n, 1), :] = jnp.max(split, axis=0, keepdims=True)

    best = None
    for q in range(quads):
        top = top_ref[q]
        for shift in (32, 16, 4, 2, 1):
            top = jnp.maximum(top, pltpu.roll(top, LANES - shift, 1))
        turned = top.T
        for i in range(QUAD):
            found = turned[64 * (i // 2) + 8 * (i % 2) : 64 * (i // 2) + 8 * (i % 2) + 1]
            gain_ref[QUAD * q + i : QUAD * q + i + 1] = found
            best = found if best is None else jnp.maximum(best, found)
    best_ref[...] = jnp.broadcast_to(best, best_ref.shape)


def finish_kernel(own_ref, all_ref, gain_ref, best_ref):
    gain_ref[...] = own_ref[...]
    best_ref[...] = jnp.max(all_ref[...], axis=0, keepdims=True)


def on_device(features, cut_points, grad, hess, node_ids):
    parts = lax.axis_size("row")
    others = parts * lax.axis_size("feat")
    rows, feats = features.shape
    own = feats // parts
    bins = cut_points.shape[1]
    length = (own + 3) * rows // LANES
    in_vmem = pl.BlockSpec(memory_space=pltpu.VMEM)
    sent = pl.pallas_call(
        sort_kernel,
        out_shape=jax.ShapeDtypeStruct((parts, length, LANES), jnp.bfloat16),
        in_specs=[pl.BlockSpec(memory_space=pltpu.MemorySpace.HBM)] * 4,
        out_specs=in_vmem,
        scratch_shapes=[
            pltpu.VMEM((rows, feats), jnp.bfloat16),
            pltpu.VMEM((1, rows), jnp.float32),
            pltpu.VMEM((1, rows), jnp.float32),
            pltpu.VMEM((1, rows), jnp.int32),
            pltpu.SemaphoreType.DMA((4,)),
        ],
        name="sort_rows",
        compiler_params=pltpu.CompilerParams(vmem_limit_bytes=67043328),
    )(features, grad[None], hess[None], node_ids[None])
    gathered = lax.all_to_all(sent, "row", 0, 0)
    edges = lax.dynamic_slice_in_dim(cut_points, lax.axis_index("row") * own, own, 0)
    tile_rows = PIECE * parts
    feature_gain, best = pl.pallas_call(
        gain_kernel,
        out_shape=(
            jax.ShapeDtypeStruct((own, NODES), jnp.float32),
            jax.ShapeDtypeStruct((others, NODES), jnp.float32),
        ),
        in_specs=[in_vmem] * 2,
        out_specs=(in_vmem, in_vmem),
        scratch_shapes=[
            pltpu.VMEM((parts, 24, LANES), jnp.float32),
            pltpu.VMEM((8, own, LANES), jnp.float32),
            *[
                pltpu.VMEM((LANES // PIECE, height, tile_rows), jnp.float32)
                for height in (own, own, 8, own, own, 8)
            ],
            pltpu.VMEM((LANES // PIECE, own // QUAD, QUAD * FINE, tile_rows), jnp.bfloat16),
            pltpu.VMEM((LANES // PIECE, PAIRED, 2 * QUAD * FINE, tile_rows), jnp.bfloat16),
            pltpu.VMEM((LANES // PIECE, own // 2, 2 * COARSE, tile_rows), jnp.bfloat16),
            pltpu.VMEM((NODES, own // QUAD, 2 * COARSE, LANES), jnp.float32),
            pltpu.VMEM((NODES, 2 * COARSE, LANES), jnp.float32),
            pltpu.VMEM((own // QUAD, NODES, LANES), jnp.float32),
        ],
        name="split_gain",
        compiler_params=pltpu.CompilerParams(vmem_limit_bytes=40 << 20),
    )(gathered, edges)
    feature_gain, node_best = pl.pallas_call(
        finish_kernel,
        out_shape=(
            jax.ShapeDtypeStruct((own, NODES), jnp.float32),
            jax.ShapeDtypeStruct((1, NODES), jnp.float32),
        ),
        in_specs=[in_vmem] * 2,
        out_specs=(in_vmem, in_vmem),
        name="write_gains",
        compiler_params=pltpu.CompilerParams(vmem_limit_bytes=4 << 20),
    )(feature_gain, lax.all_to_all(best, ("row", "feat"), 0, 0))
    return (feature_gain, node_best[0])


def solution(mesh):
    placed = (P("row", "feat"), P("feat", None), P("row"), P("row"), P("row"))
    return jax.shard_map(
        on_device,
        mesh=mesh,
        in_specs=placed,
        out_specs=(P(("feat", "row"), None), P()),
        check_vma=False,
    )
```

```python
import jax
import jax.numpy as jnp
from jax import lax
from jax.experimental import pallas as pl
from jax.experimental.pallas import tpu as pltpu
from jax.sharding import PartitionSpec as P

NODES = 32
PENALTY = 1.0
LANES = 128
COARSE = 8
FINE = 32
PIECE = 32
QUAD = 4
NODE_BLOCK = 4
PAIRED = (0, 2)


def dot_nt(left, right):
    return lax.dot_general(
        left, right, (((1,), (1,)), ((), ())), preferred_element_type=jnp.float32
    )


def iota(shape, axis):
    return lax.broadcasted_iota(jnp.int32, shape, axis)


def look_up(table, index):
    return jnp.take_along_axis(table, index, axis=1, mode="promise_in_bounds")


def sort_kernel(
    value_in, grad_in, hess_in, node_in, sent_ref, value_ref, grad_ref, hess_ref, node_ref, arrived
):
    pairs = ((node_in, node_ref), (grad_in, grad_ref), (hess_in, hess_ref), (value_in, value_ref))
    copies = [
        pltpu.make_async_copy(source, target, arrived.at[k])
        for k, (source, target) in enumerate(pairs)
    ]
    for copy in copies:
        copy.start()
    rows, feats = value_ref.shape
    parts = sent_ref.shape[0]
    own = feats // parts
    chunks = rows // LANES
    copies[0].wait()
    node = node_ref[...]
    member = (jnp.broadcast_to(node, (NODES, rows)) == iota((NODES, rows), 0)).astype(jnp.float32)
    earlier = (jnp.broadcast_to(node, (NODES, rows)) < iota((NODES, rows), 0)).astype(jnp.float32)
    upper = (iota((LANES, LANES), 0) <= iota((LANES, LANES), 1)).astype(jnp.bfloat16)
    offset = jnp.sum(earlier, axis=1, keepdims=True)
    ranks = []
    for c in range(chunks):
        piece = member[:, c * LANES : (c + 1) * LANES]
        running = jnp.dot(piece.astype(jnp.bfloat16), upper, preferred_element_type=jnp.float32)
        ranks.append(jnp.sum(piece * (running + (offset - 1.0)), axis=0, keepdims=True))
        offset = offset + jnp.sum(piece, axis=1, keepdims=True)
    rank = jnp.concatenate(ranks, axis=1).astype(jnp.int32)

    for copy in copies[1:]:
        copy.wait()
    side = jnp.concatenate(
        [grad_ref[...], hess_ref[...], node.astype(jnp.float32), jnp.zeros((13, rows), jnp.float32)],
        axis=0,
    ).astype(jnp.bfloat16)
    operand = jnp.concatenate([value_ref[...].T, side], axis=0)
    block = 2 * LANES
    sides = []
    for b in range(rows // block):
        chosen = jnp.where(
            jnp.broadcast_to(rank, (block, rows)) == iota((block, rows), 0) + b * block, 1.0, 0.0
        ).astype(jnp.bfloat16)
        moved = dot_nt(operand, chosen)
        for half in range(2):
            c = 2 * b + half
            lanes = slice(half * LANES, (half + 1) * LANES)
            sent_ref[:, c * own : (c + 1) * own, :] = (
                moved[:feats, lanes].astype(jnp.bfloat16).reshape(parts, own, LANES)
            )
            sides.append(moved[feats : feats + 3, lanes])
    packed = jnp.concatenate(
        [sides[c][i : i + 1] for i in range(3) for c in range(chunks)], axis=0
    ).astype(jnp.bfloat16)
    for d in range(parts):
        sent_ref[d, chunks * own :, :] = packed


def search_tables(edges):
    feats = edges.shape[0]
    lane = iota((feats, LANES), 1)
    low, high = edges[:, :LANES], edges[:, LANES:]

    def pick(index):
        place = jnp.where(index >= LANES, index - LANES, index)
        return jnp.where(
            index >= LANES,
            look_up(high, place),
            look_up(low, place),
        )

    inner = jnp.zeros((feats, LANES), jnp.int32)
    for level in range(7):
        start = 1 << level
        inner = jnp.where(lane >= start, (2 * (lane - start) + 1) * (1 << (7 - level)), inner)
    return pick(inner), pick(2 * lane + 1)


def gain_kernel(
    sent_ref, edge_ref, gain_ref, best_ref,
    side_ref, wide_edge_ref, even_fine_ref, even_coarse_ref, even_side_ref,
    odd_fine_ref, odd_coarse_ref, odd_side_ref,
    stat_ref, paired_ref, wide_ref, hist_ref, total_ref, top_ref,
):
    parts = sent_ref.shape[0]
    feats, bins = edge_ref.shape
    chunks = (sent_ref.shape[1] - 24) // feats
    per_vector = LANES // PIECE
    tile_rows = even_fine_ref.shape[2]
    quads = feats // QUAD

    hist_ref[...] = jnp.zeros_like(hist_ref)
    total = jnp.zeros((16, NODES), jnp.float32)
    for s in range(parts):
        side = sent_ref[s, chunks * feats :, :].astype(jnp.float32)
        side_ref[s] = side
        for c in range(0, chunks, 2):
            grad, hess, node = [
                jnp.concatenate([side[8 * i + c : 8 * i + c + 1], side[8 * i + c + 1 : 8 * i + c + 2]], axis=1)
                for i in range(3)
            ]
            wide = (NODES, 2 * LANES)
            member = jnp.where(
                jnp.broadcast_to(node, wide).astype(jnp.bfloat16)
                == iota(wide, 0).astype(jnp.float32).astype(jnp.bfloat16),
                jnp.bfloat16(1),
                jnp.bfloat16(0),
            )
            both = jnp.concatenate(
                [jnp.broadcast_to(grad, (8, 2 * LANES)), jnp.broadcast_to(hess, (8, 2 * LANES))], axis=0
            ).astype(jnp.bfloat16)
            total = total + dot_nt(both, member)
    spread = jnp.concatenate([total, jnp.zeros((16, LANES - NODES), jnp.float32)], axis=1)
    for n in range(NODES):
        total_ref[n] = jnp.broadcast_to(spread[:, n : n + 1], (16, LANES))

    edges = edge_ref[...]
    inner, leaf = search_tables(edges)

    for j in range(8):
        wide_edge_ref[j] = jnp.broadcast_to(edges[:, 32 * j : 32 * j + 1], (feats, LANES))

    def search(value):
        bits = []
        for level in range(3):
            choice = [wide_edge_ref[(2 * m + 1) << (2 - level)] for m in range(1 << level)]
            for bit in reversed(bits):
                choice = [
                    jnp.where(bit, choice[2 * m + 1], choice[2 * m])
                    for m in range(len(choice) // 2)
                ]
            bits.append(value >= choice[0])
        place = jnp.where(bits[0], 12, 8)
        for level in range(1, 3):
            place = place + jnp.where(bits[level], 4 >> level, 0)
        for level in range(3, 8):
            if level < 7:
                edge = look_up(inner, place)
            else:
                edge = look_up(leaf, place - LANES)
            place = place + place + jnp.where(value >= edge, 1, 0)
        return jnp.where(value >= wide_edge_ref[0], place - 256, -1)

    def shuffle(pieces, block):
        pieces = list(pieces)
        step = per_vector // 2
        while step >= 1:
            keep = (block & step) == 0
            for s in range(per_vector):
                if s & step == 0:
                    a, b = pieces[s], pieces[s + step]
                    pieces[s] = jnp.where(keep, a, pltpu.roll(b, step * PIECE, 1))
                    pieces[s + step] = jnp.where(keep, pltpu.roll(a, LANES - step * PIECE, 1), b)
            step //= 2
        return pieces

    block = iota((feats, LANES), 1) // PIECE
    block_side = iota((3, LANES), 1) // PIECE

    def prepare(c, fine_ref, coarse_ref, side_tile_ref):
        least, most = [None] * per_vector, [None] * per_vector
        for q in range(parts // per_vector):
            slots, sides = [], []
            for s in range(q * per_vector, (q + 1) * per_vector):
                value = sent_ref[s, pl.ds(pl.multiple_of(c * feats, feats), feats), :]
                slots.append(search(value.astype(jnp.float32)))
                sides.append(side_ref[s, pl.ds(c, 3, stride=8), :])
            lanes = slice(q * LANES, (q + 1) * LANES)
            for j, slot in enumerate(shuffle(slots, block)):
                coarse_ref[j, :, lanes] = (slot >> 5).astype(jnp.float32)
                fine_ref[j, :, lanes] = (slot & 31).astype(jnp.float32)
            for j, side in enumerate(shuffle(sides, block_side)):
                side_tile_ref[j, 0:3, lanes] = side
                node = side[2:3]
                least[j] = node if q == 0 else jnp.minimum(least[j], node)
                most[j] = node if q == 0 else jnp.maximum(most[j], node)
        return [
            (
                jnp.minimum(jnp.min(least[j]).astype(jnp.int32), NODES - NODE_BLOCK),
                jnp.max(most[j]).astype(jnp.int32),
            )
            for j in range(per_vector)
        ]

    deep = 2 * COARSE
    pair_rows = (deep, tile_rows)
    step_index = (iota(pair_rows, 0) & 7).astype(jnp.float32)
    fine_index = [(step_index + 8.0 * j).astype(jnp.bfloat16) for j in range(FINE // 8)]
    coarse_index = step_index.astype(jnp.bfloat16)
    quarter_lane = iota((COARSE, LANES), 1)
    quarter = ((quarter_lane >> 6) << 1) | ((quarter_lane >> 3) & 1)
    zero = jnp.bfloat16(0)
    one = jnp.bfloat16(1)
    two = jnp.bfloat16(2)

    def mask_nodes(first, count, node_wide, both):
        return [
            jnp.where(node_wide == (first + b).astype(jnp.float32).astype(jnp.bfloat16), part, zero)
            for b in range(count)
            for part in both
        ]

    def add_product(u, q, first, masked):
        here = [wide_ref[u, q * (QUAD // 2) + i] for i in range(QUAD // 2)]
        stream = jnp.concatenate([h * m for m in masked for h in here], axis=0)
        product = dot_nt(stream, stat_ref[u, q])
        for k in range(len(masked)):
            add_block(first + k // 2, q, k % 2, product[k * 32 : k * 32 + 32])

    def add_block(n, q, k, part):
        packed = part[:COARSE]
        for i in range(1, QUAD):
            packed = jnp.where(quarter == i, part[COARSE * i : COARSE * (i + 1)], packed)
        hist_ref[n, q, k * COARSE : (k + 1) * COARSE] += packed

    def add_paired(u, q, first, masked):
        here = [wide_ref[u, q * (QUAD // 2) + i] for i in range(QUAD // 2)]
        stream = jnp.concatenate([h * m for m in masked for h in here], axis=0)
        product = dot_nt(stream, paired_ref[u, PAIRED.index(q)])
        for k in range(len(masked)):
            for odd in range(2):
                add_block(
                    first + 2 * (k // 2) + odd, q, k % 2,
                    product[k * 32 : k * 32 + 32, odd * LANES : (odd + 1) * LANES],
                )

    def tile_sides(side_tile_ref, u):
        grad, hess, node = [
            jnp.broadcast_to(side_tile_ref[u, k : k + 1, :], pair_rows).astype(jnp.bfloat16)
            for k in range(3)
        ]
        return node, (grad, hess)

    def pair_of(ref, u, f):
        return jnp.concatenate(
            [
                jnp.broadcast_to(ref[u, f + k : f + k + 1, :], (COARSE, tile_rows))
                for k in range(2)
            ],
            axis=0,
        ).astype(jnp.bfloat16)

    def accumulate(ranges, fine_ref, coarse_ref, side_tile_ref):
        for u in range(per_vector):
            node_wide, both = tile_sides(side_tile_ref, u)
            first = ranges[u][0]
            masked = mask_nodes(first, NODE_BLOCK, node_wide, both)
            place = node_wide - first.astype(jnp.float32).astype(jnp.bfloat16)
            second = place >= two
            coupled = [jnp.where(second, zero, part) for part in both] + [
                jnp.where(second, part, zero) for part in both
            ]
            parity = [
                jnp.where(place == jnp.bfloat16(k), one, jnp.where(place == jnp.bfloat16(k + 2), one, zero))
                for k in range(2)
            ]
            for q in range(quads):
                for i in range(QUAD // 2):
                    f = q * QUAD + 2 * i
                    fine = pair_of(fine_ref, u, f)
                    for j in range(FINE // 8):
                        at = i * 2 * FINE + deep * j
                        inside = fine <= fine_index[j]
                        if q not in PAIRED:
                            stat_ref[u, q, at : at + deep, :] = jnp.where(inside, one, zero)
                        else:
                            for k in range(2):
                                low = k * LANES + at
                                paired_ref[u, PAIRED.index(q), low : low + deep, :] = (
                                    jnp.where(inside, parity[k], zero)
                                )
                    coarse = pair_of(coarse_ref, u, f)
                    wide_ref[u, f // 2] = jnp.where(coarse == coarse_index, one, zero)
                if q not in PAIRED:
                    add_product(u, q, first, masked)
                else:
                    add_paired(u, q, first, coupled)

    def accumulate_rest(ranges, fine_ref, side_tile_ref):
        most = ranges[0][1] - ranges[0][0]
        for first, last in ranges[1:]:
            most = jnp.maximum(most, last - first)

        @pl.when(most >= NODE_BLOCK)
        def _():
            for u in range(per_vector):
                tile_rest(u, *ranges[u], fine_ref, side_tile_ref)

    def tile_rest(u, first, last, fine_ref, side_tile_ref):
        @pl.loop(first + NODE_BLOCK, last + 1)
        def _(n):
            node_wide, both = tile_sides(side_tile_ref, u)
            masked = mask_nodes(n, 1, node_wide, both)
            for q in range(quads):
                if q in PAIRED:
                    for i in range(QUAD // 2):
                        fine = pair_of(fine_ref, u, q * QUAD + 2 * i)
                        for j in range(FINE // 8):
                            at = i * 2 * FINE + deep * j
                            stat_ref[u, q, at : at + deep, :] = jnp.where(
                                fine <= fine_index[j], one, zero
                            )
                add_product(u, q, n, masked)

    even = (even_fine_ref, even_coarse_ref, even_side_ref)
    odd = (odd_fine_ref, odd_coarse_ref, odd_side_ref)

    def two_chunks(pair, ranges):
        accumulate(ranges, *even)
        later = prepare(2 * pair + 1, *odd)
        accumulate_rest(ranges, even_fine_ref, even_side_ref)
        accumulate(later, *odd)
        following = prepare(jnp.minimum(2 * pair + 2, chunks - 1), *even)
        accumulate_rest(later, odd_fine_ref, odd_side_ref)
        return following

    lax.fori_loop(0, chunks // 2, two_chunks, prepare(0, *even))

    row = iota((COARSE, LANES), 0)
    last_lane = iota((COARSE, LANES), 1) | 55

    def left_sums(part):
        ends = look_up(part, last_lane)
        shift = 1
        while shift < COARSE:
            ends = ends + jnp.where(row >= shift, pltpu.roll(ends, shift, 0), 0.0)
            shift *= 2
        return part + jnp.where(row >= 1, pltpu.roll(ends, 1, 0), 0.0)

    @pl.loop(0, NODES // 4)
    def _(group):
        for k in range(4):
            n = 4 * group + k
            grad_total = total_ref[n, :COARSE]
            hess_total = total_ref[n, COARSE:]
            whole = jnp.square(grad_total) / (hess_total + PENALTY)
            for q in range(quads):
                part = hist_ref[n, q]
                grad_left = left_sums(part[:COARSE])
                hess_left = left_sums(part[COARSE:])
                split = jnp.square(grad_left) / (hess_left + PENALTY)
                split = split + jnp.square(grad_total - grad_left) / (
                    hess_total - hess_left + PENALTY
                )
                split = split - whole
                top_ref[q, pl.ds(n, 1), :] = jnp.max(split, axis=0, keepdims=True)

    best = None
    for q in range(quads):
        top = top_ref[q]
        for shift in (32, 16, 4, 2, 1):
            top = jnp.maximum(top, pltpu.roll(top, LANES - shift, 1))
        turned = top.T
        for i in range(QUAD):
            found = turned[64 * (i // 2) + 8 * (i % 2) : 64 * (i // 2) + 8 * (i % 2) + 1]
            gain_ref[QUAD * q + i : QUAD * q + i + 1] = found
            best = found if best is None else jnp.maximum(best, found)
    best_ref[...] = jnp.broadcast_to(best, best_ref.shape)


def finish_kernel(own_ref, all_ref, gain_ref, best_ref):
    gain_ref[...] = own_ref[...]
    best_ref[...] = jnp.max(all_ref[...], axis=0, keepdims=True)


def on_device(features, cut_points, grad, hess, node_ids):
    parts = lax.axis_size("row")
    others = parts * lax.axis_size("feat")
    rows, feats = features.shape
    own = feats // parts
    bins = cut_points.shape[1]
    length = (own + 3) * rows // LANES
    in_vmem = pl.BlockSpec(memory_space=pltpu.VMEM)
    sent = pl.pallas_call(
        sort_kernel,
        out_shape=jax.ShapeDtypeStruct((parts, length, LANES), jnp.bfloat16),
        in_specs=[pl.BlockSpec(memory_space=pltpu.MemorySpace.HBM)] * 4,
        out_specs=in_vmem,
        scratch_shapes=[
            pltpu.VMEM((rows, feats), jnp.bfloat16),
            pltpu.VMEM((1, rows), jnp.float32),
            pltpu.VMEM((1, rows), jnp.float32),
            pltpu.VMEM((1, rows), jnp.int32),
            pltpu.SemaphoreType.DMA((4,)),
        ],
        name="sort_rows",
        compiler_params=pltpu.CompilerParams(vmem_limit_bytes=67043328),
    )(features, grad[None], hess[None], node_ids[None])
    gathered = lax.all_to_all(sent, "row", 0, 0)
    edges = lax.dynamic_slice_in_dim(cut_points, lax.axis_index("row") * own, own, 0)
    tile_rows = PIECE * parts
    feature_gain, best = pl.pallas_call(
        gain_kernel,
        out_shape=(
            jax.ShapeDtypeStruct((own, NODES), jnp.float32),
            jax.ShapeDtypeStruct((others, NODES), jnp.float32),
        ),
        in_specs=[in_vmem] * 2,
        out_specs=(in_vmem, in_vmem),
        scratch_shapes=[
            pltpu.VMEM((parts, 24, LANES), jnp.float32),
            pltpu.VMEM((8, own, LANES), jnp.float32),
            *[
                pltpu.VMEM((LANES // PIECE, height, tile_rows), jnp.float32)
                for height in (own, own, 8, own, own, 8)
            ],
            pltpu.VMEM((LANES // PIECE, own // QUAD, QUAD * FINE, tile_rows), jnp.bfloat16),
            pltpu.VMEM((LANES // PIECE, len(PAIRED), 2 * QUAD * FINE, tile_rows), jnp.bfloat16),
            pltpu.VMEM((LANES // PIECE, own // 2, 2 * COARSE, tile_rows), jnp.bfloat16),
            pltpu.VMEM((NODES, own // QUAD, 2 * COARSE, LANES), jnp.float32),
            pltpu.VMEM((NODES, 2 * COARSE, LANES), jnp.float32),
            pltpu.VMEM((own // QUAD, NODES, LANES), jnp.float32),
        ],
        name="split_gain",
        compiler_params=pltpu.CompilerParams(vmem_limit_bytes=40 << 20),
    )(gathered, edges)
    feature_gain, node_best = pl.pallas_call(
        finish_kernel,
        out_shape=(
            jax.ShapeDtypeStruct((own, NODES), jnp.float32),
            jax.ShapeDtypeStruct((1, NODES), jnp.float32),
        ),
        in_specs=[in_vmem] * 2,
        out_specs=(in_vmem, in_vmem),
        name="write_gains",
        compiler_params=pltpu.CompilerParams(vmem_limit_bytes=4 << 20),
    )(feature_gain, lax.all_to_all(best, ("row", "feat"), 0, 0))
    return (feature_gain, node_best[0])


def solution(mesh):
    placed = (P("row", "feat"), P("feat", None), P("row"), P("row"), P("row"))
    return jax.shard_map(
        on_device,
        mesh=mesh,
        in_specs=placed,
        out_specs=(P(("feat", "row"), None), P()),
        check_vma=False,
    )
```

```python
import jax
import jax.numpy as jnp
from jax import lax
from jax.experimental import pallas as pl
from jax.experimental.pallas import tpu as pltpu
from jax.sharding import PartitionSpec as P

NODES = 32
PENALTY = 1.0
LANES = 128
COARSE = 8
FINE = 32
PIECE = 32
QUAD = 4
NODE_BLOCK = 4
PAIRED = (1, 3)


def dot_nt(left, right):
    return lax.dot_general(
        left, right, (((1,), (1,)), ((), ())), preferred_element_type=jnp.float32
    )


def iota(shape, axis):
    return lax.broadcasted_iota(jnp.int32, shape, axis)


def look_up(table, index):
    return jnp.take_along_axis(table, index, axis=1, mode="promise_in_bounds")


def sort_kernel(
    value_in, grad_in, hess_in, node_in, sent_ref, value_ref, grad_ref, hess_ref, node_ref, arrived
):
    pairs = ((node_in, node_ref), (grad_in, grad_ref), (hess_in, hess_ref), (value_in, value_ref))
    copies = [
        pltpu.make_async_copy(source, target, arrived.at[k])
        for k, (source, target) in enumerate(pairs)
    ]
    for copy in copies:
        copy.start()
    rows, feats = value_ref.shape
    parts = sent_ref.shape[0]
    own = feats // parts
    chunks = rows // LANES
    copies[0].wait()
    node = node_ref[...]
    member = (jnp.broadcast_to(node, (NODES, rows)) == iota((NODES, rows), 0)).astype(jnp.float32)
    earlier = (jnp.broadcast_to(node, (NODES, rows)) < iota((NODES, rows), 0)).astype(jnp.float32)
    upper = (iota((LANES, LANES), 0) <= iota((LANES, LANES), 1)).astype(jnp.bfloat16)
    offset = jnp.sum(earlier, axis=1, keepdims=True)
    ranks = []
    for c in range(chunks):
        piece = member[:, c * LANES : (c + 1) * LANES]
        running = jnp.dot(piece.astype(jnp.bfloat16), upper, preferred_element_type=jnp.float32)
        ranks.append(jnp.sum(piece * (running + (offset - 1.0)), axis=0, keepdims=True))
        offset = offset + jnp.sum(piece, axis=1, keepdims=True)
    rank = jnp.concatenate(ranks, axis=1).astype(jnp.int32)

    for copy in copies[1:]:
        copy.wait()
    side = jnp.concatenate(
        [grad_ref[...], hess_ref[...], node.astype(jnp.float32), jnp.zeros((13, rows), jnp.float32)],
        axis=0,
    ).astype(jnp.bfloat16)
    operand = jnp.concatenate([value_ref[...].T, side], axis=0)
    block = 2 * LANES
    sides = []
    for b in range(rows // block):
        chosen = jnp.where(
            jnp.broadcast_to(rank, (block, rows)) == iota((block, rows), 0) + b * block, 1.0, 0.0
        ).astype(jnp.bfloat16)
        moved = dot_nt(operand, chosen)
        for half in range(2):
            c = 2 * b + half
            lanes = slice(half * LANES, (half + 1) * LANES)
            sent_ref[:, c * own : (c + 1) * own, :] = (
                moved[:feats, lanes].astype(jnp.bfloat16).reshape(parts, own, LANES)
            )
            sides.append(moved[feats : feats + 3, lanes])
    packed = jnp.concatenate(
        [sides[c][i : i + 1] for i in range(3) for c in range(chunks)], axis=0
    ).astype(jnp.bfloat16)
    for d in range(parts):
        sent_ref[d, chunks * own :, :] = packed


def search_tables(edges):
    feats = edges.shape[0]
    lane = iota((feats, LANES), 1)
    low, high = edges[:, :LANES], edges[:, LANES:]

    def pick(index):
        place = jnp.where(index >= LANES, index - LANES, index)
        return jnp.where(
            index >= LANES,
            look_up(high, place),
            look_up(low, place),
        )

    inner = jnp.zeros((feats, LANES), jnp.int32)
    for level in range(7):
        start = 1 << level
        inner = jnp.where(lane >= start, (2 * (lane - start) + 1) * (1 << (7 - level)), inner)
    return pick(inner), pick(2 * lane + 1)


def gain_kernel(
    sent_ref, edge_ref, gain_ref, best_ref,
    side_ref, wide_edge_ref, even_fine_ref, even_coarse_ref, even_side_ref,
    odd_fine_ref, odd_coarse_ref, odd_side_ref,
    stat_ref, paired_ref, wide_ref, hist_ref, total_ref, top_ref,
):
    parts = sent_ref.shape[0]
    feats, bins = edge_ref.shape
    chunks = (sent_ref.shape[1] - 24) // feats
    per_vector = LANES // PIECE
    tile_rows = even_fine_ref.shape[2]
    quads = feats // QUAD

    hist_ref[...] = jnp.zeros_like(hist_ref)
    total = jnp.zeros((16, NODES), jnp.float32)
    for s in range(parts):
        side = sent_ref[s, chunks * feats :, :].astype(jnp.float32)
        side_ref[s] = side
        for c in range(0, chunks, 2):
            grad, hess, node = [
                jnp.concatenate([side[8 * i + c : 8 * i + c + 1], side[8 * i + c + 1 : 8 * i + c + 2]], axis=1)
                for i in range(3)
            ]
            wide = (NODES, 2 * LANES)
            member = jnp.where(
                jnp.broadcast_to(node, wide).astype(jnp.bfloat16)
                == iota(wide, 0).astype(jnp.float32).astype(jnp.bfloat16),
                jnp.bfloat16(1),
                jnp.bfloat16(0),
            )
            both = jnp.concatenate(
                [jnp.broadcast_to(grad, (8, 2 * LANES)), jnp.broadcast_to(hess, (8, 2 * LANES))], axis=0
            ).astype(jnp.bfloat16)
            total = total + dot_nt(both, member)
    spread = jnp.concatenate([total, jnp.zeros((16, LANES - NODES), jnp.float32)], axis=1)
    for n in range(NODES):
        total_ref[n] = jnp.broadcast_to(spread[:, n : n + 1], (16, LANES))

    edges = edge_ref[...]
    inner, leaf = search_tables(edges)

    for j in range(8):
        wide_edge_ref[j] = jnp.broadcast_to(edges[:, 32 * j : 32 * j + 1], (feats, LANES))

    def search(value):
        bits = []
        for level in range(3):
            choice = [wide_edge_ref[(2 * m + 1) << (2 - level)] for m in range(1 << level)]
            for bit in reversed(bits):
                choice = [
                    jnp.where(bit, choice[2 * m + 1], choice[2 * m])
                    for m in range(len(choice) // 2)
                ]
            bits.append(value >= choice[0])
        place = jnp.where(bits[0], 12, 8)
        for level in range(1, 3):
            place = place + jnp.where(bits[level], 4 >> level, 0)
        for level in range(3, 8):
            if level < 7:
                edge = look_up(inner, place)
            else:
                edge = look_up(leaf, place - LANES)
            place = place + place + jnp.where(value >= edge, 1, 0)
        return jnp.where(value >= wide_edge_ref[0], place - 256, -1)

    def shuffle(pieces, block):
        pieces = list(pieces)
        step = per_vector // 2
        while step >= 1:
            keep = (block & step) == 0
            for s in range(per_vector):
                if s & step == 0:
                    a, b = pieces[s], pieces[s + step]
                    pieces[s] = jnp.where(keep, a, pltpu.roll(b, step * PIECE, 1))
                    pieces[s + step] = jnp.where(keep, pltpu.roll(a, LANES - step * PIECE, 1), b)
            step //= 2
        return pieces

    block = iota((feats, LANES), 1) // PIECE
    block_side = iota((3, LANES), 1) // PIECE

    def prepare(c, fine_ref, coarse_ref, side_tile_ref):
        least, most = [None] * per_vector, [None] * per_vector
        for q in range(parts // per_vector):
            slots, sides = [], []
            for s in range(q * per_vector, (q + 1) * per_vector):
                value = sent_ref[s, pl.ds(pl.multiple_of(c * feats, feats), feats), :]
                slots.append(search(value.astype(jnp.float32)))
                sides.append(side_ref[s, pl.ds(c, 3, stride=8), :])
            lanes = slice(q * LANES, (q + 1) * LANES)
            for j, slot in enumerate(shuffle(slots, block)):
                coarse_ref[j, :, lanes] = (slot >> 5).astype(jnp.float32)
                fine_ref[j, :, lanes] = (slot & 31).astype(jnp.float32)
            for j, side in enumerate(shuffle(sides, block_side)):
                side_tile_ref[j, 0:3, lanes] = side
                node = side[2:3]
                least[j] = node if q == 0 else jnp.minimum(least[j], node)
                most[j] = node if q == 0 else jnp.maximum(most[j], node)
        return [
            (
                jnp.minimum(jnp.min(least[j]).astype(jnp.int32), NODES - NODE_BLOCK),
                jnp.max(most[j]).astype(jnp.int32),
            )
            for j in range(per_vector)
        ]

    deep = 2 * COARSE
    pair_rows = (deep, tile_rows)
    step_index = (iota(pair_rows, 0) & 7).astype(jnp.float32)
    fine_index = [(step_index + 8.0 * j).astype(jnp.bfloat16) for j in range(FINE // 8)]
    coarse_index = step_index.astype(jnp.bfloat16)
    quarter_lane = iota((COARSE, LANES), 1)
    quarter = ((quarter_lane >> 6) << 1) | ((quarter_lane >> 3) & 1)
    zero = jnp.bfloat16(0)
    one = jnp.bfloat16(1)
    two = jnp.bfloat16(2)

    def mask_nodes(first, count, node_wide, both):
        return [
            jnp.where(node_wide == (first + b).astype(jnp.float32).astype(jnp.bfloat16), part, zero)
            for b in range(count)
            for part in both
        ]

    def add_product(u, q, first, masked):
        here = [wide_ref[u, q * (QUAD // 2) + i] for i in range(QUAD // 2)]
        stream = jnp.concatenate([h * m for m in masked for h in here], axis=0)
        product = dot_nt(stream, stat_ref[u, q])
        for k in range(len(masked)):
            add_block(first + k // 2, q, k % 2, product[k * 32 : k * 32 + 32])

    def add_block(n, q, k, part):
        packed = part[:COARSE]
        for i in range(1, QUAD):
            packed = jnp.where(quarter == i, part[COARSE * i : COARSE * (i + 1)], packed)
        hist_ref[n, q, k * COARSE : (k + 1) * COARSE] += packed

    def add_paired(u, q, first, masked):
        here = [wide_ref[u, q * (QUAD // 2) + i] for i in range(QUAD // 2)]
        stream = jnp.concatenate([h * m for m in masked for h in here], axis=0)
        product = dot_nt(stream, paired_ref[u, PAIRED.index(q)])
        for k in range(len(masked)):
            for odd in range(2):
                add_block(
                    first + 2 * (k // 2) + odd, q, k % 2,
                    product[k * 32 : k * 32 + 32, odd * LANES : (odd + 1) * LANES],
                )

    def tile_sides(side_tile_ref, u):
        grad, hess, node = [
            jnp.broadcast_to(side_tile_ref[u, k : k + 1, :], pair_rows).astype(jnp.bfloat16)
            for k in range(3)
        ]
        return node, (grad, hess)

    def pair_of(ref, u, f):
        return jnp.concatenate(
            [
                jnp.broadcast_to(ref[u, f + k : f + k + 1, :], (COARSE, tile_rows))
                for k in range(2)
            ],
            axis=0,
        ).astype(jnp.bfloat16)

    def accumulate(ranges, fine_ref, coarse_ref, side_tile_ref):
        for u in range(per_vector):
            node_wide, both = tile_sides(side_tile_ref, u)
            first = ranges[u][0]
            masked = mask_nodes(first, NODE_BLOCK, node_wide, both)
            place = node_wide - first.astype(jnp.float32).astype(jnp.bfloat16)
            second = place >= two
            coupled = [jnp.where(second, zero, part) for part in both] + [
                jnp.where(second, part, zero) for part in both
            ]
            parity = [
                jnp.where(place == jnp.bfloat16(k), one, jnp.where(place == jnp.bfloat16(k + 2), one, zero))
                for k in range(2)
            ]
            for q in range(quads):
                for i in range(QUAD // 2):
                    f = q * QUAD + 2 * i
                    fine = pair_of(fine_ref, u, f)
                    for j in range(FINE // 8):
                        at = i * 2 * FINE + deep * j
                        inside = fine <= fine_index[j]
                        if q not in PAIRED:
                            stat_ref[u, q, at : at + deep, :] = jnp.where(inside, one, zero)
                        else:
                            for k in range(2):
                                low = k * LANES + at
                                paired_ref[u, PAIRED.index(q), low : low + deep, :] = (
                                    jnp.where(inside, parity[k], zero)
                                )
                    coarse = pair_of(coarse_ref, u, f)
                    wide_ref[u, f // 2] = jnp.where(coarse == coarse_index, one, zero)
                if q not in PAIRED:
                    add_product(u, q, first, masked)
                else:
                    add_paired(u, q, first, coupled)

    def accumulate_rest(ranges, fine_ref, side_tile_ref):
        most = ranges[0][1] - ranges[0][0]
        for first, last in ranges[1:]:
            most = jnp.maximum(most, last - first)

        @pl.when(most >= NODE_BLOCK)
        def _():
            for u in range(per_vector):
                tile_rest(u, *ranges[u], fine_ref, side_tile_ref)

    def tile_rest(u, first, last, fine_ref, side_tile_ref):
        @pl.loop(first + NODE_BLOCK, last + 1)
        def _(n):
            node_wide, both = tile_sides(side_tile_ref, u)
            masked = mask_nodes(n, 1, node_wide, both)
            for q in range(quads):
                if q in PAIRED:
                    for i in range(QUAD // 2):
                        fine = pair_of(fine_ref, u, q * QUAD + 2 * i)
                        for j in range(FINE // 8):
                            at = i * 2 * FINE + deep * j
                            stat_ref[u, q, at : at + deep, :] = jnp.where(
                                fine <= fine_index[j], one, zero
                            )
                add_product(u, q, n, masked)

    even = (even_fine_ref, even_coarse_ref, even_side_ref)
    odd = (odd_fine_ref, odd_coarse_ref, odd_side_ref)

    def two_chunks(pair, ranges):
        accumulate(ranges, *even)
        later = prepare(2 * pair + 1, *odd)
        accumulate_rest(ranges, even_fine_ref, even_side_ref)
        accumulate(later, *odd)
        following = prepare(jnp.minimum(2 * pair + 2, chunks - 1), *even)
        accumulate_rest(later, odd_fine_ref, odd_side_ref)
        return following

    lax.fori_loop(0, chunks // 2, two_chunks, prepare(0, *even))

    row = iota((COARSE, LANES), 0)
    last_lane = iota((COARSE, LANES), 1) | 55

    def left_sums(part):
        ends = look_up(part, last_lane)
        shift = 1
        while shift < COARSE:
            ends = ends + jnp.where(row >= shift, pltpu.roll(ends, shift, 0), 0.0)
            shift *= 2
        return part + jnp.where(row >= 1, pltpu.roll(ends, 1, 0), 0.0)

    @pl.loop(0, NODES // 4)
    def _(group):
        for k in range(4):
            n = 4 * group + k
            grad_total = total_ref[n, :COARSE]
            hess_total = total_ref[n, COARSE:]
            whole = jnp.square(grad_total) / (hess_total + PENALTY)
            for q in range(quads):
                part = hist_ref[n, q]
                grad_left = left_sums(part[:COARSE])
                hess_left = left_sums(part[COARSE:])
                split = jnp.square(grad_left) / (hess_left + PENALTY)
                split = split + jnp.square(grad_total - grad_left) / (
                    hess_total - hess_left + PENALTY
                )
                split = split - whole
                top_ref[q, pl.ds(n, 1), :] = jnp.max(split, axis=0, keepdims=True)

    best = None
    for q in range(quads):
        top = top_ref[q]
        for shift in (32, 16, 4, 2, 1):
            top = jnp.maximum(top, pltpu.roll(top, LANES - shift, 1))
        turned = top.T
        for i in range(QUAD):
            found = turned[64 * (i // 2) + 8 * (i % 2) : 64 * (i // 2) + 8 * (i % 2) + 1]
            gain_ref[QUAD * q + i : QUAD * q + i + 1] = found
            best = found if best is None else jnp.maximum(best, found)
    best_ref[...] = jnp.broadcast_to(best, best_ref.shape)


def finish_kernel(own_ref, all_ref, gain_ref, best_ref):
    gain_ref[...] = own_ref[...]
    best_ref[...] = jnp.max(all_ref[...], axis=0, keepdims=True)


def on_device(features, cut_points, grad, hess, node_ids):
    parts = lax.axis_size("row")
    others = parts * lax.axis_size("feat")
    rows, feats = features.shape
    own = feats // parts
    bins = cut_points.shape[1]
    length = (own + 3) * rows // LANES
    in_vmem = pl.BlockSpec(memory_space=pltpu.VMEM)
    sent = pl.pallas_call(
        sort_kernel,
        out_shape=jax.ShapeDtypeStruct((parts, length, LANES), jnp.bfloat16),
        in_specs=[pl.BlockSpec(memory_space=pltpu.MemorySpace.HBM)] * 4,
        out_specs=in_vmem,
        scratch_shapes=[
            pltpu.VMEM((rows, feats), jnp.bfloat16),
            pltpu.VMEM((1, rows), jnp.float32),
            pltpu.VMEM((1, rows), jnp.float32),
            pltpu.VMEM((1, rows), jnp.int32),
            pltpu.SemaphoreType.DMA((4,)),
        ],
        name="sort_rows",
        compiler_params=pltpu.CompilerParams(vmem_limit_bytes=67043328),
    )(features, grad[None], hess[None], node_ids[None])
    gathered = lax.all_to_all(sent, "row", 0, 0)
    edges = lax.dynamic_slice_in_dim(cut_points, lax.axis_index("row") * own, own, 0)
    tile_rows = PIECE * parts
    feature_gain, best = pl.pallas_call(
        gain_kernel,
        out_shape=(
            jax.ShapeDtypeStruct((own, NODES), jnp.float32),
            jax.ShapeDtypeStruct((others, NODES), jnp.float32),
        ),
        in_specs=[in_vmem] * 2,
        out_specs=(in_vmem, in_vmem),
        scratch_shapes=[
            pltpu.VMEM((parts, 24, LANES), jnp.float32),
            pltpu.VMEM((8, own, LANES), jnp.float32),
            *[
                pltpu.VMEM((LANES // PIECE, height, tile_rows), jnp.float32)
                for height in (own, own, 8, own, own, 8)
            ],
            pltpu.VMEM((LANES // PIECE, own // QUAD, QUAD * FINE, tile_rows), jnp.bfloat16),
            pltpu.VMEM((LANES // PIECE, len(PAIRED), 2 * QUAD * FINE, tile_rows), jnp.bfloat16),
            pltpu.VMEM((LANES // PIECE, own // 2, 2 * COARSE, tile_rows), jnp.bfloat16),
            pltpu.VMEM((NODES, own // QUAD, 2 * COARSE, LANES), jnp.float32),
            pltpu.VMEM((NODES, 2 * COARSE, LANES), jnp.float32),
            pltpu.VMEM((own // QUAD, NODES, LANES), jnp.float32),
        ],
        name="split_gain",
        compiler_params=pltpu.CompilerParams(vmem_limit_bytes=40 << 20),
    )(gathered, edges)
    feature_gain, node_best = pl.pallas_call(
        finish_kernel,
        out_shape=(
            jax.ShapeDtypeStruct((own, NODES), jnp.float32),
            jax.ShapeDtypeStruct((1, NODES), jnp.float32),
        ),
        in_specs=[in_vmem] * 2,
        out_specs=(in_vmem, in_vmem),
        name="write_gains",
        compiler_params=pltpu.CompilerParams(vmem_limit_bytes=4 << 20),
    )(feature_gain, lax.all_to_all(best, ("row", "feat"), 0, 0))
    return (feature_gain, node_best[0])


def solution(mesh):
    placed = (P("row", "feat"), P("feat", None), P("row"), P("row"), P("row"))
    return jax.shard_map(
        on_device,
        mesh=mesh,
        in_specs=placed,
        out_specs=(P(("feat", "row"), None), P()),
        check_vma=False,
    )
```
